512 devices in a mesh: req: 128 (over x, z, core), tp: 4 (over y).
Axes of the slice: x: 4, y: 4, z: 16, core: 2. Of those that a mesh axis runs over, the one named last changes fastest.
Arguments:
- queries: bfloat16 [2, 128, 32, 1536], P(None, 'req', None, 'tp')
- response_kv: bfloat16 [2, 128, 2, 32, 256], P(None, 'req'), may hold values from -6 to 6
- cache_kv: bfloat16 [2, 128, 2, 384, 256], P(None, 'req'), may hold values from -6 to 6
- residual: bfloat16 [2, 128, 32, 1536], P(None, 'req')
- out_proj: bfloat16 [2, 1536, 1536], P(None, 'tp'), may hold values from -0.5 to 0.5
- norm_gain: float32 [2, 1536], replicated, may hold values from 0.25 to 1.75
- lm_head: bfloat16 [2, 131072, 1536], P(None, 'req', 'tp')
- targets: int32 [128, 32], P(None, 'tp'), may hold values from 0 to 131071
- resp_lengths: int32 [128], replicated, may hold values from 1 to 32, 2560 in all
- cache_lengths: int32 [128], P('req'), may hold values from 1 to 384, 30720 in all
- owner_slot: int32 [128], replicated, may hold values from 0 to 127, each once
- sink_count: int32 [1], replicated, may hold values from 1 to 95
- window_size: int32 [1], replicated, may hold values from 48 to 191
Outputs:
- token_logprobs: float32 [128, 32], P('req', 'tp')
- request_scores: float32 [128, 2], P('req')
The draws below stay inside these ranges and needn't reach their ends.
Inputs may be any that keep to these rules, and one draw needn't show every extreme that they name: `resp_lengths`: live response slots are the first ones; all lengths sum to 2560. `cache_lengths`: live cache slots are the first ones; all lengths sum to 30720. `owner_slot`: A permutation of the requests.
All inputs are finite; a program needn't handle non-finite values. No bound on the sum of `cache_lengths` on one device may be relied on, other than what follows from the above.
Results may differ from the reference program's by a relative error of at most 0.0014.
Values may be sent and summed in bfloat16 or wider, within the bound.
A program may use at most 128 MiB of HBM per device.

```python
import math
import jax
import jax.numpy as jnp
import numpy as np
from jax import lax

D = 1536
HEADS = 12
HEAD = 128
KV_HEADS = 2
VOCAB_REQ = 1024
RESP = 32
CACHE = 384
REQS = 128
VOCAB = 131072
N_REQ = 128


def draw_residual(key, part):
    key_base, key_rows, key_cols = jax.random.split(key, 3)
    base_value = jnp.clip(jax.random.normal(key_base, (2, REQS, RESP, D), jnp.float32), -6.0, 6.0)
    row_low = 0.3
    row_high = 3.0
    row_scale = jnp.exp(jax.random.uniform(key_rows, (2, REQS, RESP, 1), jnp.float32, math.log(row_low), math.log(row_high)))
    col_scale = jnp.exp(jax.random.uniform(key_cols, (2, 1, 1, D), jnp.float32, math.log(0.3), math.log(3.0)))
    return (base_value * row_scale * col_scale).astype(jnp.bfloat16)


def draw_queries(key, part):
    key_base = jax.random.fold_in(key, 0)
    base_value = jnp.clip(jax.random.normal(key_base, (2, REQS, RESP, HEADS, HEAD), jnp.float32), -6.0, 6.0)
    return base_value.reshape(2, REQS, RESP, HEADS * HEAD).astype(jnp.bfloat16)


def draw_lm_head(key, part):
    key_base = jax.random.fold_in(key, 0)
    base_value = jnp.clip(jax.random.normal(key_base, (2, VOCAB, D), jnp.float32), -6.0, 6.0) * (3.0 / math.sqrt(D))
    return base_value.astype(jnp.bfloat16)


def with_ends(values, own_key, smallest, top_value):
    index_at = [jax.random.randint(jax.random.fold_in(own_key, axis), (), 0, length) for axis, length in enumerate(values.shape)]
    main_axis = values.shape.index(max(values.shape))
    neighbour = index_at[:main_axis] + [(index_at[main_axis] + 1) % values.shape[main_axis]] + index_at[main_axis + 1:]
    return values.at[tuple(index_at)].set(smallest).at[tuple(neighbour)].set(top_value)


def block_scale(own_key, dims, cuts, low, largest):
    gain = 1.0
    for position, parts in cuts:
        heights = jax.random.uniform(jax.random.fold_in(jax.random.fold_in(own_key, 6), position), (parts,), jnp.float32, low / len(cuts), largest / len(cuts))
        gain = gain * jnp.repeat(jnp.exp(heights), dims[position] // parts).reshape((-1,) + (1,) * (len(dims) - 1 - position))
    return gain


def profile(count, total, most, skew):
    loads = [(1 << 20) // math.isqrt(rank ** skew) + 1 for rank in range(2, count + 1)]
    surplus, holding = total - most - (count - 1), [1] * (count - 1)
    while surplus > 0:
        movable = [i for i in range(count - 1) if holding[i] < most]
        whole, budget = sum([loads[i] for i in movable]), surplus
        for i in movable:
            more = min(most - holding[i], max(1, budget * loads[i] // whole), surplus)
            holding[i] = holding[i] + more
            surplus = surplus - more
    return np.array([most] + holding)


def uneven_parts(own_key, count, total, limit, lean):
    if count == 2:
        one = jax.random.randint(own_key, (), max(1, total - limit), min(limit, total - 1) + 1)
        return jnp.stack([one, total - one])
    sizes = jnp.asarray(profile(count, total, limit, lean), jnp.int32)
    couples = (count - 1) // 2
    source_of, sink = sizes[1:1 + 2 * couples:2], sizes[2:2 + 2 * couples:2]
    margin = jnp.minimum(source_of - 1, limit - sink)
    passed = jax.random.randint(jax.random.fold_in(own_key, 1), (couples,), 0, 1 << 20) % (margin + 1)
    sizes = sizes.at[1:1 + 2 * couples:2].set(source_of - passed).at[2:2 + 2 * couples:2].set(sink + passed)
    return sizes[jax.random.permutation(jax.random.fold_in(own_key, 2), count)]


def bell_draw(own_key, extent, spread, most, cuts=(), kind=jnp.bfloat16):
    gain = block_scale(own_key, extent, cuts, -0.22, 0.18) if cuts else 1.0
    result = jax.random.normal(own_key, extent, jnp.float32) * spread * gain
    return jnp.minimum(jnp.maximum(result, -most), most).astype(kind)


def setup_inputs(seed: int = 0) -> dict:
    key_of = jax.random.split(jax.random.key(seed), 14)
    return {
        "queries": draw_queries(jax.random.fold_in(key_of[13], 71), 0),
        "response_kv": bell_draw(key_of[1], (2, REQS, 2, RESP, KV_HEADS * HEAD), 1.0, 6.0, ((1, 128),)),
        "cache_kv": bell_draw(key_of[2], (2, REQS, 2, CACHE, KV_HEADS * HEAD), 1.0, 6.0, ((1, 128),)),
        "residual": draw_residual(jax.random.fold_in(key_of[13], 71), 0),
        "out_proj": bell_draw(key_of[4], (2, HEADS * HEAD, D), HEAD ** -0.5, 0.5, ((1, 4),)),
        "norm_gain": jnp.clip(1.0 + 0.15 * jax.random.normal(key_of[5], (2, D), jnp.float32), 0.25, 1.75),
        "lm_head": draw_lm_head(jax.random.fold_in(key_of[13], 71), 0),
        "targets": with_ends(jax.random.randint(key_of[7], (REQS, RESP), 0, VOCAB), jax.random.fold_in(key_of[7], 1), 0, VOCAB - 1).astype(jnp.int32),
        "resp_lengths": uneven_parts(key_of[8], REQS, REQS * RESP * 5 // 8, RESP, 2).astype(jnp.int32),
        "cache_lengths": uneven_parts(key_of[9], REQS, REQS * CACHE * 5 // 8, CACHE, 2).astype(jnp.int32),
        "owner_slot": jax.random.permutation(key_of[10], REQS).astype(jnp.int32),
        "sink_count": jax.random.randint(key_of[11], (1,), 1, CACHE // 4).astype(jnp.int32),
        "window_size": jax.random.randint(key_of[12], (1,), CACHE // 8, CACHE // 2).astype(jnp.int32),
    }


def span_mask(lengths, sink_count, window_size):
    cache_pos = jnp.arange(CACHE, dtype=jnp.int32)
    slot_pos = jnp.arange(RESP, dtype=jnp.int32)
    req_count = lengths.shape[0]
    key_pos = jnp.concatenate([jnp.broadcast_to(cache_pos[None, :], (req_count, CACHE)), lengths[:, None] + slot_pos[None, :]], axis=1)
    key_live = jnp.concatenate([cache_pos[None, :] < lengths[:, None], jnp.ones((req_count, RESP), jnp.bool_)], axis=1)
    query_pos = lengths[:, None] + slot_pos[None, :]
    earlier = key_pos[:, None, :] <= query_pos[:, :, None]
    inside = (key_pos[:, None, :] < sink_count[0]) | (query_pos[:, :, None] - key_pos[:, None, :] < window_size[0])
    return key_live[:, None, :] & earlier & inside

def attend(queries, response_kv, cache_kv, cache_lengths, sink_count, window_size):
    group_size = HEADS // KV_HEADS
    key_span = CACHE + RESP
    query_heads = queries.astype(jnp.float32).reshape(2, REQS, RESP, KV_HEADS, group_size, HEAD)
    key_rows = jnp.concatenate([cache_kv[:, :, 0], response_kv[:, :, 0]], axis=2).astype(jnp.float32).reshape(2, REQS, key_span, KV_HEADS, HEAD)
    value_rows = jnp.concatenate([cache_kv[:, :, 1], response_kv[:, :, 1]], axis=2).astype(jnp.float32).reshape(2, REQS, key_span, KV_HEADS, HEAD)
    scores = jnp.einsum('mrsgjd,mrkgd->mrgjsk', query_heads, key_rows) * HEAD ** (-0.5)
    allowed = span_mask(cache_lengths, sink_count, window_size)[None, :, None, None]
    masked = jnp.where(allowed, scores, -jnp.inf)
    row_peak = lax.optimization_barrier(jnp.max(masked, axis=-1, keepdims=True))
    weights = jnp.exp(masked - row_peak)
    weights = (weights / lax.optimization_barrier(jnp.sum(weights, axis=-1, keepdims=True))).astype(jnp.bfloat16)
    attended = jnp.einsum('mrgjsk,mrkgd->mrsgjd', weights.astype(jnp.float32), value_rows)
    return attended.astype(jnp.bfloat16).reshape(2, REQS, RESP, HEADS * HEAD)

def rms_norm(hidden, norm_gain):
    scale_inv = lax.rsqrt(lax.optimization_barrier(jnp.mean(hidden * hidden, axis=-1, keepdims=True)) + 1e-06)
    return (hidden * scale_inv * norm_gain[:, None, None, :]).astype(jnp.bfloat16)

def vocab_logprob(flat_rows, lm_head, flat_targets):
    rows_wide = flat_rows.astype(jnp.float32)
    row_total = flat_rows.shape[1]
    blocks = lm_head.reshape(2, N_REQ, VOCAB_REQ, D).transpose(1, 0, 2, 3)
    block_starts = jnp.arange(N_REQ, dtype=jnp.int32) * VOCAB_REQ

    def scan_step(running, inputs):
        run_peak, run_total, run_picked = running
        head_block, block_start = inputs
        logits = jnp.einsum('mtd,mvd->mtv', rows_wide, head_block.astype(jnp.float32))
        new_peak = jnp.maximum(run_peak, lax.optimization_barrier(jnp.max(logits, axis=-1)))
        exp_total = run_total * jnp.exp(run_peak - new_peak) + lax.optimization_barrier(jnp.sum(jnp.exp(logits - new_peak[..., None]), axis=-1))
        target_hits = (block_start + jnp.arange(VOCAB_REQ, dtype=jnp.int32))[None, None, :] == flat_targets[None, :, None]
        picked = run_picked + lax.optimization_barrier(jnp.sum(jnp.where(target_hits, logits, 0.0), axis=-1))
        return ((new_peak, exp_total, picked), None)
    initial = (jnp.full((2, row_total), -jnp.inf, jnp.float32), jnp.zeros((2, row_total), jnp.float32), jnp.zeros((2, row_total), jnp.float32))
    final_state, ignored = lax.scan(scan_step, initial, (blocks, block_starts))
    run_peak, run_total, run_picked = final_state
    return run_picked - (run_peak + jnp.log(run_total))

def reference(queries, response_kv, cache_kv, residual, out_proj, norm_gain, lm_head, targets, resp_lengths, cache_lengths, owner_slot, sink_count, window_size):
    attended = attend(queries, response_kv, cache_kv, cache_lengths, sink_count, window_size)
    projected = jnp.einsum('mrsf,mfd->mrsd', attended.astype(jnp.float32), out_proj.astype(jnp.float32))
    hidden = residual.astype(jnp.float32) + projected
    normed = rms_norm(hidden, norm_gain)
    logprob = vocab_logprob(normed.reshape(2, REQS * RESP, D), lm_head, targets.reshape(-1)).reshape(2, REQS, RESP)
    row_order = jnp.zeros((REQS,), jnp.int32).at[owner_slot].set(jnp.arange(REQS, dtype=jnp.int32))
    placed = logprob[:, row_order]
    lengths_placed = resp_lengths[row_order]
    live_slots = jnp.arange(RESP, dtype=jnp.int32)[None, :] < lengths_placed[:, None]
    policy = jnp.where(live_slots, placed[0], 0.0)
    log_ratio = jnp.where(live_slots, placed[0] - placed[1], 0.0)
    counts = lengths_placed.astype(jnp.float32)
    request_scores = jnp.stack([lax.optimization_barrier(jnp.sum(policy, axis=1)) / counts, lax.optimization_barrier(jnp.sum(log_ratio, axis=1)) / counts], axis=1)
    return (policy, request_scores)
```

```python
import jax
import jax.numpy as jnp
from jax import lax
from jax.experimental import pallas as pl
from jax.experimental.pallas import tpu as pltpu
from jax.sharding import PartitionSpec as P

HEADS = 12
HEAD = 128
KV_HEADS = 2
RESP = 32
CACHE = 384
D = 1536

NX, NZ, NC, NT = 4, 16, 2, 4
REQS = NX * NZ * NC
SLOTS = 16
FEAT = D // NT
VOCAB_BLOCK = 1024
PIECES = 4
PIECE = VOCAB_BLOCK // PIECES
MESH = pl.DeviceIdType.MESH
EXACT = lax.Precision.HIGHEST


def span_mask(lengths, sink_count, window_size):
    cache_pos = jnp.arange(CACHE, dtype=jnp.int32)
    slot_pos = jnp.arange(RESP, dtype=jnp.int32)
    req_count = lengths.shape[0]
    key_pos = jnp.concatenate([cache_pos[None, :], lengths[:, None] + slot_pos[None, :]], axis=1)
    key_live = jnp.concatenate(
        [cache_pos[None, :] < lengths[:, None], jnp.ones((req_count, RESP), jnp.bool_)], axis=1
    )
    query_pos = lengths[:, None] + slot_pos[None, :]
    earlier = key_pos[:, None, :] <= query_pos[:, :, None]
    inside = (key_pos[:, None, :] < sink_count[0]) | (
        query_pos[:, :, None] - key_pos[:, None, :] < window_size[0]
    )
    return key_live[:, None, :] & earlier & inside


def iota(shape, dim):
    return lax.broadcasted_iota(jnp.int32, shape, dim)


def nt_dot(a, b, precision=None):
    return lax.dot_general(
        a, b, (((1,), (1,)), ((), ())), precision=precision, preferred_element_type=jnp.float32
    )


def fused(
    partial, residual, gain, head, targets, lengths, owner,
    policy_out, scores_out,
    hbuf, rows, rs_in, tgt_in, tgt_all, own_all, xbuf, outbuf, in1, ex2, in2, lpbuf, in3,
    local_sem, rs_s, rs_r, tg_s, tg_r, hp_s, hp_r, hq_s, hq_r, hf_s, hf_r,
    x_s, x_r, zr_s, zr_r, zl_s, zl_r, cr_s, cr_r, cl_s, cl_r, e1_s, e1_r, e2_s, e2_r, e3_s, e3_r,
):
    req = lax.axis_index("req")
    t = lax.axis_index("tp")
    x = req // (NZ * NC)
    z = (req // NC) % NZ
    c = req % NC
    model = t // 2
    half = t % 2
    pair = t + 1 - 2 * (t % 2)
    across = NT - 1 - t

    def index_of(px, pz, pc):
        return (px * NZ + pz) * NC + pc

    def send(src, dst, ssem, rsem, preq, pt):
        return pltpu.make_async_remote_copy(
            src_ref=src, dst_ref=dst, send_sem=ssem, recv_sem=rsem,
            device_id={"req": preq, "tp": pt}, device_id_type=MESH,
        )

    barrier = pltpu.get_barrier_semaphore()

    def greet(preq, pt):
        pl.semaphore_signal(
            barrier, inc=1, device_id={"req": preq, "tp": pt}, device_id_type=MESH
        )

    for d in range(1, NT):
        greet(req, (t + d) % NT)
    group = x * NC + c
    for d in range(1, NX * NC):
        other = (group + d) % (NX * NC)
        greet(index_of(other // NC, z, other % NC), t)
    for d in range(1, NZ):
        greet(index_of(x, (z + d) % NZ, c), t)
    pl.semaphore_wait(barrier, (NT - 1) + (NX * NC - 1) + (NZ - 1))

    def rs_copy(d):
        pt = (t + d) % NT
        start = pl.multiple_of((pt % 2) * SLOTS, SLOTS)
        return send(
            partial.at[pt // 2, pl.ds(start, SLOTS)], rs_in.at[d], rs_s.at[d], rs_r.at[d], req, pt
        )

    for d in range(1, NT):
        rs_copy(d).start()

    def lanes(source):
        return pl.ds(pl.multiple_of(source * FEAT, FEAT), FEAT)

    def piece(k):
        return pl.ds(k * PIECE, PIECE)

    def pair_copy(k):
        return send(
            head.at[model, piece(k)], hbuf.at[piece(k), lanes(t)], hp_s.at[k], hp_r.at[k], req, pair
        )

    def across_copy(k):
        return send(
            head.at[1 - model, piece(k)], hbuf.at[piece(k), lanes(t)], hq_s.at[k], hq_r.at[k],
            req, across,
        )

    def across_recv(k):
        return send(
            head.at[1 - model, piece(k)], hbuf.at[piece(k), lanes(across)], hq_s.at[k], hq_r.at[k],
            req, across,
        )

    def forward_copy(k):
        part = hbuf.at[piece(k), lanes(across)]
        return send(part, part, hf_s.at[k], hf_r.at[k], req, pair)

    def pair_recv(k):
        part = hbuf.at[piece(k), lanes(pair)]
        return send(part, part, hp_s.at[k], hp_r.at[k], req, pair)

    def forward_recv(k):
        part = hbuf.at[piece(k), lanes(NT - 1 - pair)]
        return send(part, part, hf_s.at[k], hf_r.at[k], req, pair)

    for k in range(PIECES):
        across_copy(k).start()
        pair_copy(k).start()
    own_head = pltpu.make_async_copy(head.at[model], hbuf.at[:, lanes(t)], local_sem)
    own_head.start()

    req_sub = iota((REQS, 128), 0)
    lane_l = iota((REQS, 128), 1)
    same_xc = ((req_sub >> 5) == (lane_l >> 5)) & ((req_sub & 1) == ((lane_l >> 4) & 1))
    same_z = ((iota((NZ, REQS), 1) >> 1) & (NZ - 1)) == iota((NZ, REQS), 0)
    zmask = jnp.where(same_z, 1.0, 0.0)
    spread = jnp.where(
        (iota((8, 128), 1) & (SLOTS - 1)) == iota((8, 128), 0) + 8 * half, 1.0, 0.0
    )
    wide = jnp.dot(
        targets[...].astype(jnp.float32), spread, precision=EXACT,
        preferred_element_type=jnp.float32,
    )
    placed = jnp.dot(
        zmask, jnp.where(same_xc, wide, 0.0), precision=EXACT, preferred_element_type=jnp.float32
    )
    tgt_in[0] = placed.astype(jnp.int32)

    def tgt_copy(d):
        return send(tgt_in.at[0], tgt_in.at[d], tg_s.at[d], tg_r.at[d], req, (t + d) % NT)

    for d in range(1, NT):
        tgt_copy(d).start()
    own_all[...] = jnp.dot(
        zmask * owner[...].astype(jnp.float32), jnp.where(same_xc, 1.0, 0.0), precision=EXACT,
        preferred_element_type=jnp.float32,
    ).astype(jnp.int32)
    outbuf[...] = jnp.zeros_like(outbuf)

    start = pl.multiple_of(half * SLOTS, SLOTS)
    hidden = residual[model, pl.ds(start, SLOTS), :].astype(jnp.float32)
    total = partial[model, pl.ds(start, SLOTS), :]
    for d in range(1, NT):
        rs_copy(d).wait_recv()
        total = total + rs_in[d]
    hidden = hidden + total
    scale_inv = lax.rsqrt(jnp.mean(hidden * hidden, axis=-1, keepdims=True) + 1e-06)
    rows[x, z, c] = (hidden * scale_inv * gain[pl.ds(model, 1), :]).astype(jnp.bfloat16)

    def x_copy(d):
        part = rows.at[x, z, c]
        return send(part, part, x_s.at[d], x_r.at[d], index_of((x + d) % NX, z, c), t)

    def x_recv(d):
        part = rows.at[(x + NX - d) % NX, z, c]
        return send(part, part, x_s.at[d], x_r.at[d], index_of((x + NX - d) % NX, z, c), t)

    for d in range(1, NX):
        x_copy(d).start()
    for d in range(1, NX):
        x_recv(d).wait_recv()

    right = index_of(x, (z + 1) % NZ, c)
    left = index_of(x, (z + NZ - 1) % NZ, c)
    twin = index_of(x, z, 1 - c)

    def right_copy(s):
        part = rows.at[:, (z + NZ - s) % NZ, c]
        return send(part, part, zr_s.at[s], zr_r.at[s], right, t)

    def right_recv(s):
        part = rows.at[:, (z + NZ - s - 1) % NZ, c]
        return send(part, part, zr_s.at[s], zr_r.at[s], right, t)

    def left_copy(s):
        part = rows.at[:, (z + s) % NZ, c]
        return send(part, part, zl_s.at[s], zl_r.at[s], left, t)

    def left_recv(s):
        part = rows.at[:, (z + s + 1) % NZ, c]
        return send(part, part, zl_s.at[s], zl_r.at[s], left, t)

    def twin_right(s):
        part = rows.at[:, (z + NZ - s) % NZ, c]
        return send(part, part, cr_s.at[s], cr_r.at[s], twin, t)

    def twin_left(s):
        part = rows.at[:, (z + s % 8) % NZ, c]
        return send(part, part, cl_s.at[s], cl_r.at[s], twin, t)

    def twin_right_recv(s):
        part = rows.at[:, (z + NZ - s) % NZ, 1 - c]
        return send(part, part, cr_s.at[s], cr_r.at[s], twin, t)

    def twin_left_recv(s):
        part = rows.at[:, (z + s % 8) % NZ, 1 - c]
        return send(part, part, cl_s.at[s], cl_r.at[s], twin, t)

    right_copy(0).start()
    left_copy(0).start()
    twin_left(8).start()

    tgt_own = jnp.zeros((NZ, 128), jnp.int32)
    for d in range(NT):
        if d:
            tgt_copy(d).wait_recv()
        wanted_half = ((t + NT - d) % NT) // 2 == half
        tgt_own = tgt_own + jnp.where(wanted_half, tgt_in[d], 0)
    tgt_all[...] = tgt_own - req * VOCAB_BLOCK

    def ring_step(s):
        right_recv(s - 1).wait_recv()
        right_copy(s).start()
        twin_right(s).start()
        left_recv(s - 1).wait_recv()

        @pl.when(s < 7)
        def _():
            left_copy(s).start()

        twin_left(s).start()

    def first_steps(s, carry):
        ring_step(s)
        across_recv(s - 1).wait_recv()
        forward_copy(s - 1).start()
        return carry

    lax.fori_loop(1, 5, first_steps, 0)

    own_head.wait()

    def head_wait(k, carry):
        pair_recv(k).wait_recv()
        forward_recv(k).wait_recv()
        return carry

    lax.fori_loop(0, PIECES, head_wait, 0)

    def block_rows(pz):
        return rows[:, pz].reshape(NX * NC * SLOTS, D)

    def compute(k):
        z1 = (z + NZ - k) % NZ
        z2 = (z + k % 8) % NZ
        twin_right_recv(k).wait_recv()
        twin_left_recv(k).wait_recv()
        xbuf[0:128] = block_rows(z1)
        xbuf[128:256] = block_rows(z2)
        logits = nt_dot(hbuf[...], xbuf[...])
        peak = jnp.max(logits, axis=0, keepdims=True)
        norm = jnp.sum(jnp.exp(logits - peak), axis=0, keepdims=True)
        lse = peak + jnp.log(norm)
        wanted = jnp.concatenate([tgt_all[pl.ds(z1, 1), :], tgt_all[pl.ds(z2, 1), :]], axis=1)
        hit = iota((VOCAB_BLOCK, 256), 0) == wanted
        pick = jnp.sum(jnp.where(hit, logits, 0.0), axis=0, keepdims=True)
        sub = iota((128, 128), 0)
        slot = iota((128, 128), 1) & (SLOTS - 1)
        dest = ((sub >> 5) * NZ + (sub & (NZ - 1))) * NC + ((sub >> 4) & 1)
        found = jnp.zeros((128, 128), jnp.float32)
        for i, pz in enumerate((z1, z2)):
            cols = slice(128 * i, 128 * i + 128)
            values = jnp.where(
                sub == slot, lse[:, cols], jnp.where(sub == slot + SLOTS, pick[:, cols], 0.0)
            )
            select = jnp.where(dest == own_all[pl.ds(pz, 1), :], 1.0, 0.0)
            found = found + nt_dot(select, values, EXACT)
        outbuf[...] += found

    def late_steps(s, carry):
        ring_step(s)
        compute(2 * s - 9)
        compute(2 * s - 8)
        return carry

    lax.fori_loop(5, 8, late_steps, 0)
    right_recv(7).wait_recv()
    twin_right(8).start()

    def last_chunks(k, carry):
        compute(k)
        return carry

    lax.fori_loop(7, 9, last_chunks, 0)

    def e1_copy(d):
        other = (group + d) % (NX * NC)
        return send(
            outbuf.at[pl.ds(pl.multiple_of(other * NZ, NZ), NZ)], in1.at[d], e1_s.at[d], e1_r.at[d],
            index_of(other // NC, z, other % NC), t,
        )

    for d in range(1, NX * NC):
        e1_copy(d).start()
    in1[0] = outbuf[pl.ds(pl.multiple_of(group * NZ, NZ), NZ), :]
    for d in range(1, NX * NC):
        e1_copy(d).wait_recv()

    def combine(values):
        peak = jnp.max(values, axis=0, keepdims=True)
        lse = peak + jnp.log(jnp.sum(jnp.exp(values - peak), axis=0, keepdims=True))
        pick = jnp.sum(values, axis=0, keepdims=True)
        return jnp.where(iota(lse.shape, 2) < SLOTS, lse, pick)[0]

    merged = combine(in1[...])
    for k in range(NZ):
        ex2[k] = merged[k : k + 1]

    def e2_copy(d):
        pz = (z + d) % NZ
        return send(ex2.at[pz], in2.at[d], e2_s.at[d], e2_r.at[d], index_of(x, pz, c), t)

    for d in range(1, NZ):
        e2_copy(d).start()
    in2[0] = ex2[z]
    for d in range(1, NZ):
        e2_copy(d).wait_recv()
    final = combine(in2[...])
    logprob = pltpu.roll(final, 128 - SLOTS, 1) - final
    lpbuf[...] = logprob
    in3[t] = logprob

    def e3_copy(d):
        return send(lpbuf, in3.at[t], e3_s.at[d], e3_r.at[d], req, (t + d) % NT)

    def e3_recv(d):
        return send(lpbuf, in3.at[(t + NT - d) % NT], e3_s.at[d], e3_r.at[d], req, (t + d) % NT)

    for d in range(1, NT):
        e3_copy(d).start()
    count = jnp.sum(jnp.where(owner[...] == req, lengths[...], 0), axis=1, keepdims=True)
    for d in range(1, NT):
        e3_recv(d).wait_recv()
    lane = iota((1, 128), 1)
    live0 = (lane < SLOTS) & (lane < count)
    live1 = (lane < SLOTS) & (lane + SLOTS < count)
    low, high = in3[0], in3[1]
    policy_total = jnp.sum(
        jnp.where(live0, low, 0.0) + jnp.where(live1, high, 0.0), axis=1, keepdims=True
    )
    ratio_total = jnp.sum(
        jnp.where(live0, low - in3[2], 0.0) + jnp.where(live1, high - in3[3], 0.0),
        axis=1, keepdims=True,
    )
    counts = count.astype(jnp.float32)
    scores = jnp.where(lane == 0, policy_total / counts, ratio_total / counts)
    scores_out[...] = scores[:, 0:2]
    mine = in3[t // 2]
    mine = jnp.where(half == 1, pltpu.roll(mine, 120, 1), mine)
    mine = jnp.where(lane + 8 * t < count, mine, 0.0)
    policy_out[...] = mine[:, 0:8]

    for d in range(1, NT):
        rs_copy(d).wait_send()
        tgt_copy(d).wait_send()
        x_copy(d).wait_send()
        e3_copy(d).wait_send()

    def head_sent(k, carry):
        pair_copy(k).wait_send()
        across_copy(k).wait_send()
        forward_copy(k).wait_send()
        return carry

    lax.fori_loop(0, PIECES, head_sent, 0)

    def right_sent(s, carry):
        right_copy(s).wait_send()
        twin_right(s + 1).wait_send()
        twin_left(s + 1).wait_send()
        return carry

    lax.fori_loop(0, 8, right_sent, 0)

    def left_sent(s, carry):
        left_copy(s).wait_send()
        return carry

    lax.fori_loop(0, 7, left_sent, 0)
    for d in range(1, NX * NC):
        e1_copy(d).wait_send()
    for d in range(1, NZ):
        e2_copy(d).wait_send()


def fused_call(partial, residual, gain, head, targets, lengths, owner):
    dma = pltpu.SemaphoreType.DMA
    vmem = pl.BlockSpec(memory_space=pltpu.VMEM)
    counts = [NT] * 4 + [PIECES] * 6 + [NX] * 2 + [8] * 4 + [9] * 4 + [8] * 2 + [NZ] * 2 + [NT] * 2
    return pl.pallas_call(
        fused,
        out_shape=(
            jax.ShapeDtypeStruct((1, 8), jnp.float32),
            jax.ShapeDtypeStruct((1, 2), jnp.float32),
        ),
        in_specs=[vmem, vmem, vmem, pl.BlockSpec(memory_space=pl.ANY), vmem, vmem, vmem],
        out_specs=(vmem, vmem),
        scratch_shapes=[
            pltpu.VMEM((VOCAB_BLOCK, D), jnp.bfloat16),
            pltpu.VMEM((NX, NZ, NC, SLOTS, D), jnp.bfloat16),
            pltpu.VMEM((NT, SLOTS, D), jnp.float32),
            pltpu.VMEM((NT, NZ, 128), jnp.int32),
            pltpu.VMEM((NZ, 128), jnp.int32),
            pltpu.VMEM((NZ, 128), jnp.int32),
            pltpu.VMEM((256, D), jnp.bfloat16),
            pltpu.VMEM((REQS, 128), jnp.float32),
            pltpu.VMEM((NX * NC, NZ, 128), jnp.float32),
            pltpu.VMEM((NZ, 1, 128), jnp.float32),
            pltpu.VMEM((NZ, 1, 128), jnp.float32),
            pltpu.VMEM((1, 128), jnp.float32),
            pltpu.VMEM((NT, 1, 128), jnp.float32),
            dma,
        ]
        + [dma((n,)) for n in counts],
        compiler_params=pltpu.CompilerParams(
            collective_id=0, has_side_effects=True, vmem_limit_bytes=40 << 20
        ),
    )(partial, residual, gain, head, targets, lengths, owner)


def per_device(
    queries,
    response_kv,
    cache_kv,
    residual,
    out_proj,
    norm_gain,
    lm_head,
    targets,
    resp_lengths,
    cache_lengths,
    owner_slot,
    sink_count,
    window_size,
):
    tp_size = lax.axis_size("tp")
    tp_index = lax.axis_index("tp")
    local_reqs = queries.shape[1]
    local_heads = HEADS // tp_size
    group_size = HEADS // KV_HEADS
    kv_index = tp_index * local_heads // group_size
    cache_head = lax.dynamic_slice_in_dim(cache_kv, kv_index * HEAD, HEAD, axis=4)
    resp_head = lax.dynamic_slice_in_dim(response_kv, kv_index * HEAD, HEAD, axis=4)
    key_rows = jnp.concatenate([cache_head[:, :, 0], resp_head[:, :, 0]], axis=2)
    value_rows = jnp.concatenate([cache_head[:, :, 1], resp_head[:, :, 1]], axis=2)
    query_heads = queries.reshape(2, local_reqs, RESP, local_heads, HEAD)
    scores = jnp.einsum(
        "mrshd,mrkd->mrhsk", query_heads, key_rows, preferred_element_type=jnp.float32
    ) * HEAD ** (-0.5)
    allowed = span_mask(cache_lengths, sink_count, window_size)[None, :, None]
    masked = jnp.where(allowed, scores, -jnp.inf)
    row_peak = jnp.max(masked, axis=-1, keepdims=True)
    weights = jnp.exp(masked - row_peak)
    weights = (weights / jnp.sum(weights, axis=-1, keepdims=True)).astype(jnp.bfloat16)
    attended = jnp.einsum(
        "mrhsk,mrkd->mrshd", weights, value_rows, preferred_element_type=jnp.float32
    )
    attended = attended.astype(jnp.bfloat16).reshape(2, RESP, local_heads * HEAD)
    partial = jnp.einsum("msf,mfd->msd", attended, out_proj, preferred_element_type=jnp.float32)
    return fused_call(
        partial,
        residual.reshape(2, RESP, D),
        norm_gain,
        lm_head,
        targets,
        resp_lengths.reshape(1, REQS),
        owner_slot.reshape(1, REQS),
    )


def solution(mesh):
    in_specs = (
        P(None, "req", None, "tp"),
        P(None, "req", None, None, None),
        P(None, "req", None, None, None),
        P(None, "req", None, None),
        P(None, "tp", None),
        P(),
        P(None, "req", "tp"),
        P(None, "tp"),
        P(),
        P("req"),
        P(),
        P(),
        P(),
    )
    out_specs = (P("req", "tp"), P("req", None))
    return jax.shard_map(
        per_device, mesh=mesh, in_specs=in_specs, out_specs=out_specs, check_vma=False
    )
```

```python
import jax
import jax.numpy as jnp
from jax import lax
from jax.experimental import pallas as pl
from jax.experimental.pallas import tpu as pltpu
from jax.sharding import PartitionSpec as P

HEADS = 12
HEAD = 128
KV_HEADS = 2
RESP = 32
CACHE = 384
KEYS = CACHE + RESP
D = 1536

NX, NZ, NC, NT = 4, 16, 2, 4
REQS = NX * NZ * NC
SLOTS = 16
FEAT = D // NT
GROUP = HEADS // NT
VOCAB_BLOCK = 1024
PIECES = 4
PIECE = VOCAB_BLOCK // PIECES
CHUNKS = 8
ROWS = 2 * NX * NC * SLOTS
SPLIT = 896
A = pl.ds(0, SPLIT)
B = pl.ds(SPLIT, D - SPLIT)
MESH = pl.DeviceIdType.MESH
EXACT = lax.Precision.HIGHEST


def iota(shape, dim):
    return lax.broadcasted_iota(jnp.int32, shape, dim)


def nt_dot(a, b, precision=None):
    return lax.dot_general(
        a, b, (((1,), (1,)), ((), ())), precision=precision, preferred_element_type=jnp.float32
    )


def fused(
    queries, response_kv, cache_kv, residual, out_proj, gain, head, targets, lengths, owner,
    cache_lengths, sink_count, window_size,
    policy_out, scores_out,
    qbuf, kvbuf, wbuf, resbuf, attbuf, partial,
    hbuf, rows, rs_in, tgt_in, tgt_all, own_all, wanted_buf, select_buf,
    peak_buf, norm_buf, pick_buf, outbuf, in1, ex2, in2, lpbuf, in3,
    load_sem, rs_s, rs_r, tg_s, tg_r, hp_s, hp_r, hq_s, hq_r, hf_s, hf_r,
    xa_s, xa_r, ra_s, ra_r, la_s, la_r, rb_s, rb_r, lb_s, lb_r, xb_s, xb_r,
    ca_s, ca_r, cb_s, cb_r, e1_s, e1_r, e2_s, e2_r, e3_s, e3_r,
):
    req = lax.axis_index("req")
    t = lax.axis_index("tp")
    x = req // (NZ * NC)
    z = (req // NC) % NZ
    c = req % NC
    model = t // 2
    half = t % 2
    pair = t + 1 - 2 * (t % 2)
    across = NT - 1 - t
    group = x * NC + c

    def index_of(px, pz, pc):
        return (px * NZ + pz) * NC + pc

    def send(src, dst, ssem, rsem, preq, pt):
        return pltpu.make_async_remote_copy(
            src_ref=src, dst_ref=dst, send_sem=ssem, recv_sem=rsem,
            device_id={"req": preq, "tp": pt}, device_id_type=MESH,
        )

    def lanes(source):
        return pl.ds(pl.multiple_of(source * FEAT, FEAT), FEAT)

    barrier = pltpu.get_barrier_semaphore()

    def greet(preq, pt):
        pl.semaphore_signal(
            barrier, inc=1, device_id={"req": preq, "tp": pt}, device_id_type=MESH
        )

    for d in range(1, NT):
        greet(req, (t + d) % NT)
    for d in range(1, NX * NC):
        other = (group + d) % (NX * NC)
        greet(index_of(other // NC, z, other % NC), t)
    for d in range(1, NZ):
        greet(index_of(x, (z + d) % NZ, c), t)

    kv_lanes = pl.ds(pl.multiple_of((t // 2) * HEAD, HEAD), HEAD)
    slot_start = pl.multiple_of(half * SLOTS, SLOTS)
    loads = [
        pltpu.make_async_copy(queries, qbuf, load_sem.at[0]),
        pltpu.make_async_copy(
            cache_kv.at[:, :, :, kv_lanes], kvbuf.at[:, :, pl.ds(0, CACHE)], load_sem.at[1]
        ),
        pltpu.make_async_copy(
            response_kv.at[:, :, :, kv_lanes], kvbuf.at[:, :, pl.ds(CACHE, RESP)], load_sem.at[2]
        ),
        pltpu.make_async_copy(out_proj, wbuf, load_sem.at[3]),
        pltpu.make_async_copy(residual.at[model, pl.ds(slot_start, SLOTS)], resbuf, load_sem.at[4]),
    ]
    own_head = pltpu.make_async_copy(head.at[model], hbuf.at[:, lanes(t)], load_sem.at[5])
    for copy in loads:
        copy.start()
    own_head.start()

    req_sub = iota((REQS, ROWS), 0)
    row_lane = iota((REQS, ROWS), 1)
    same_xc = ((req_sub >> 5) == (row_lane >> 6)) & ((req_sub & 1) == ((row_lane >> 4) & 1))
    same_z = ((iota((NZ, REQS), 1) >> 1) & (NZ - 1)) == iota((NZ, REQS), 0)
    zmask = jnp.where(same_z, 1.0, 0.0)

    pl.semaphore_wait(barrier, (NT - 1) + (NX * NC - 1) + (NZ - 1))

    def piece(k):
        return pl.ds(k * PIECE, PIECE)

    def pair_copy(k):
        return send(
            head.at[model, piece(k)], hbuf.at[piece(k), lanes(t)], hp_s.at[k], hp_r.at[k], req, pair
        )

    def across_copy(k):
        return send(
            head.at[1 - model, piece(k)], hbuf.at[piece(k), lanes(t)], hq_s.at[k], hq_r.at[k],
            req, across,
        )

    def across_recv(k):
        return send(
            head.at[1 - model, piece(k)], hbuf.at[piece(k), lanes(across)], hq_s.at[k], hq_r.at[k],
            req, across,
        )

    def forward_copy(k):
        part = hbuf.at[piece(k), lanes(across)]
        return send(part, part, hf_s.at[k], hf_r.at[k], req, pair)

    def pair_recv(k):
        part = hbuf.at[piece(k), lanes(pair)]
        return send(part, part, hp_s.at[k], hp_r.at[k], req, pair)

    def forward_recv(k):
        part = hbuf.at[piece(k), lanes(NT - 1 - pair)]
        return send(part, part, hf_s.at[k], hf_r.at[k], req, pair)

    across_copy(0).start()
    pair_copy(0).start()
    across_copy(1).start()

    for copy in loads[:3]:
        copy.wait()
    length = cache_lengths[0]
    stack = (GROUP * RESP, KEYS)
    query_pos = length + (iota(stack, 0) & (RESP - 1))
    key = iota(stack, 1)
    key_pos = jnp.where(key < CACHE, key, length + key - CACHE)
    key_live = (key >= CACHE) | (key < length)
    inside = (key_pos < sink_count[0]) | (query_pos - key_pos < window_size[0])
    allowed = key_live & (key_pos <= query_pos) & inside
    for m in range(2):
        stacked = jnp.concatenate(
            [qbuf[m, 0, :, HEAD * g : HEAD * g + HEAD] for g in range(GROUP)], axis=0
        )
        scores = nt_dot(stacked, kvbuf[m, 0]) * HEAD ** (-0.5)
        masked = jnp.where(allowed, scores, -jnp.inf)
        weights = jnp.exp(masked - jnp.max(masked, axis=-1, keepdims=True))
        weights = (weights / jnp.sum(weights, axis=-1, keepdims=True)).astype(jnp.bfloat16)
        attended = jnp.dot(weights, kvbuf[m, 1], preferred_element_type=jnp.float32)
        attended = attended.astype(jnp.bfloat16)
        for g in range(GROUP):
            attbuf[m, :, HEAD * g : HEAD * g + HEAD] = attended[RESP * g : RESP * g + RESP]
    loads[3].wait()
    for m in range(2):
        partial[m] = jnp.dot(attbuf[m], wbuf[m], preferred_element_type=jnp.float32)

    def rs_copy(d):
        pt = (t + d) % NT
        start = pl.multiple_of((pt % 2) * SLOTS, SLOTS)
        return send(
            partial.at[pt // 2, pl.ds(start, SLOTS)], rs_in.at[d], rs_s.at[d], rs_r.at[d], req, pt
        )

    for d in range(1, NT):
        rs_copy(d).start()

    spread = jnp.where(
        (iota((8, ROWS), 1) & (SLOTS - 1)) == iota((8, ROWS), 0) + 8 * half, 1.0, 0.0
    )
    wide = jnp.dot(
        targets[...].astype(jnp.float32), spread, precision=EXACT,
        preferred_element_type=jnp.float32,
    )
    placed = jnp.dot(
        zmask, jnp.where(same_xc, wide, 0.0), precision=EXACT, preferred_element_type=jnp.float32
    )
    tgt_in[0] = placed.astype(jnp.int32)

    def tgt_copy(d):
        return send(tgt_in.at[0], tgt_in.at[d], tg_s.at[d], tg_r.at[d], req, (t + d) % NT)

    for d in range(1, NT):
        tgt_copy(d).start()
    own_all[...] = jnp.dot(
        zmask * owner[...].astype(jnp.float32), jnp.where(same_xc, 1.0, 0.0), precision=EXACT,
        preferred_element_type=jnp.float32,
    ).astype(jnp.int32)

    def forward_head(k):
        across_recv(k).wait_recv()
        forward_copy(k).start()
        if k + 1 < PIECES:
            pair_copy(k + 1).start()

    across_copy(2).start()
    forward_head(0)
    across_copy(3).start()

    loads[4].wait()
    hidden = resbuf[...].astype(jnp.float32)
    total = partial[model, pl.ds(slot_start, SLOTS), :]
    for d in range(1, NT):
        rs_copy(d).wait_recv()
        total = total + rs_in[d]
    hidden = hidden + total
    scale_inv = lax.rsqrt(jnp.mean(hidden * hidden, axis=-1, keepdims=True) + 1e-06)
    rows[x, 7, 1, c] = (hidden * scale_inv * gain[pl.ds(model, 1), :]).astype(jnp.bfloat16)

    right = index_of(x, (z + 1) % NZ, c)
    left = index_of(x, (z + NZ - 1) % NZ, c)
    twin = index_of(x, z, 1 - c)

    def xa_copy(d):
        part = rows.at[x, 7, 1, c, :, A]
        return send(part, part, xa_s.at[d], xa_r.at[d], index_of((x + d) % NX, z, c), t)

    def xa_recv(d):
        part = rows.at[(x + NX - d) % NX, 7, 1, c, :, A]
        return send(part, part, xa_s.at[d], xa_r.at[d], index_of((x + d) % NX, z, c), t)

    def a_copy(side, s, h, first):
        src_chunk, src_place = (7, 1) if first else (s - 1, side)
        peers = pl.ds(2 * h, 2)
        ssem, rsem, to = (ra_s, ra_r, right) if side == 0 else (la_s, la_r, left)
        return send(
            rows.at[peers, src_chunk, src_place, c, :, A], rows.at[peers, s, side, c, :, A],
            ssem.at[2 * s + h], rsem.at[2 * s + h], to, t,
        )

    def b_copy(side, s, first):
        src_chunk, src_place = (7, 1) if first else (s - 1, side)
        ssem, rsem, to = (rb_s, rb_r, right) if side == 0 else (lb_s, lb_r, left)
        return send(
            rows.at[x, src_chunk, src_place, c, :, B], rows.at[x, s, side, c, :, B],
            ssem.at[s], rsem.at[s], to, t,
        )

    def xb_copy(n, d, side=None, chunk=None):
        place = pl.ds(0, 2) if side is None else pl.ds(side, 1)
        chunk = n if chunk is None else chunk
        part = rows.at[x, chunk, place, c, :, B]
        return send(
            part, part, xb_s.at[4 * n + d], xb_r.at[4 * n + d], index_of((x + d) % NX, z, c), t
        )

    def xb_recv(n, d, side=None, chunk=None):
        place = pl.ds(0, 2) if side is None else pl.ds(side, 1)
        chunk = n if chunk is None else chunk
        part = rows.at[(x + NX - d) % NX, chunk, place, c, :, B]
        return send(
            part, part, xb_s.at[4 * n + d], xb_r.at[4 * n + d], index_of((x + d) % NX, z, c), t
        )

    def twin_copy(n, ssem, rsem, part_lanes, side=None, chunk=None, core=None):
        place = pl.ds(0, 2) if side is None else pl.ds(side, 1)
        chunk = n if chunk is None else chunk
        core = c if core is None else core
        part = rows.at[:, chunk, place, core, :, part_lanes]
        return send(part, part, ssem.at[n], rsem.at[n], twin, t)

    def twin_a(n, **kw):
        return twin_copy(n, ca_s, ca_r, A, **kw)

    def twin_b(n, **kw):
        return twin_copy(n, cb_s, cb_r, B, **kw)

    OWN = dict(side=1, chunk=7)
    LAST = dict(side=0, chunk=7)

    for d in range(1, NX):
        xa_copy(d).start()
    b_copy(0, 0, True).start()
    b_copy(1, 0, True).start()
    for d in range(1, NX):
        xb_copy(8, d, **OWN).start()
    for d in range(1, NX):
        xa_recv(d).wait_recv()
    for h in range(2):
        a_copy(0, 0, h, True).start()
        a_copy(1, 0, h, True).start()
    twin_a(8, **OWN).start()
    forward_head(1)

    tgt_own = jnp.zeros((NZ, ROWS), jnp.int32)
    for d in range(NT):
        if d:
            tgt_copy(d).wait_recv()
        wanted_half = ((t + NT - d) % NT) // 2 == half
        tgt_own = tgt_own + jnp.where(wanted_half, tgt_in[d], 0)
    tgt_all[...] = tgt_own - req * VOCAB_BLOCK
    outbuf[...] = jnp.zeros_like(outbuf)
    peak_buf[...] = jnp.full_like(peak_buf, -jnp.inf)
    norm_buf[...] = jnp.zeros_like(norm_buf)
    pick_buf[...] = jnp.zeros_like(pick_buf)

    def prepare(k):
        z1 = (z + NZ - k - 1) % NZ
        z2 = (z + (k + 1) % 8) % NZ
        first = (iota((1, ROWS), 1) & 32) == 0
        wanted_buf[k] = jnp.where(first, tgt_all[pl.ds(z1, 1), :], tgt_all[pl.ds(z2, 1), :])
        sub = iota((REQS, ROWS), 0)
        dest = ((sub >> 5) * NZ + (sub & (NZ - 1))) * NC + ((sub >> 4) & 1)
        place = jnp.where(first, own_all[pl.ds(z1, 1), :], own_all[pl.ds(z2, 1), :])
        select_buf[k] = jnp.where(dest == place, 1.0, 0.0)

    def arrive(s):
        for side in range(2):
            if side == 1 and s == 8:
                continue
            for h in range(2):
                a_copy(side, s - 1, h, s == 1).wait_recv()
                if s < 8 - side:
                    a_copy(side, s, h, False).start()
            b_copy(side, s - 1, s == 1).wait_recv()
            if s < 8 - side:
                b_copy(side, s, False).start()

    def arrive_loop(s):
        for side in range(2):
            for h in range(2):
                a_copy(side, s - 1, h, False).wait_recv()
                a_copy(side, s, h, False).start()
            b_copy(side, s - 1, False).wait_recv()
            b_copy(side, s, False).start()

    def share(s):
        for d in range(1, NX):
            xb_copy(s - 1, d).start()
        twin_a(s - 1).start()

    def share_old(n, **kw):
        for d in range(1, NX):
            xb_recv(n, d, **kw).wait_recv()
        twin_b(n, **kw).start()

    arrive(1)
    share(1)
    share_old(8, **OWN)
    forward_head(2)
    prepare(0)
    prepare(1)

    arrive(2)
    share(2)
    share_old(0)
    forward_head(3)
    prepare(2)
    prepare(3)

    def middle(s, carry):
        arrive_loop(s)
        share(s)
        share_old(s - 2)
        prepare(2 * s - 2)
        prepare(2 * s - 1)
        return carry

    lax.fori_loop(3, 5, middle, 0)

    def other_core(n, **kw):
        twin_a(n, core=1 - c, **kw).wait_recv()
        twin_b(n, core=1 - c, **kw).wait_recv()

    def head_ready(k):
        pair_recv(k).wait_recv()
        forward_recv(k).wait_recv()

    def units(k0, k1, p0, p1):
        def unit(i, carry):
            k = k0 + i // (p1 - p0)
            p = p0 + i % (p1 - p0)
            base = pl.multiple_of(p * PIECE, PIECE)
            logits = nt_dot(hbuf[pl.ds(base, PIECE), :], rows[:, k].reshape(ROWS, D))
            peak = jnp.max(logits, axis=0, keepdims=True)
            hit = iota((PIECE, ROWS), 0) == wanted_buf[k] - base
            pick_buf[k] += jnp.sum(jnp.where(hit, logits, 0.0), axis=0, keepdims=True)
            old = peak_buf[k]
            new = jnp.maximum(old, peak)
            norm = jnp.sum(jnp.exp(logits - new), axis=0, keepdims=True)
            norm_buf[k] = norm_buf[k] * jnp.exp(old - new) + norm
            peak_buf[k] = new
            return carry

        lax.fori_loop(0, (k1 - k0) * (p1 - p0), unit, 0)

    arrive_loop(5)
    share(5)
    share_old(3)
    own_head.wait()
    head_ready(0)
    head_ready(1)
    for n in range(3):
        other_core(n)
    units(0, 3, 0, 2)

    arrive_loop(6)
    share(6)
    share_old(4)
    other_core(3)
    head_ready(2)
    units(3, 4, 0, 2)
    units(0, 4, 2, 3)

    arrive(7)
    share(7)
    share_old(5)
    other_core(4)
    units(4, 5, 0, 3)
    head_ready(3)
    units(0, 3, 3, 4)

    arrive(8)
    for d in range(1, NX):
        xb_copy(7, d, **LAST).start()
    twin_a(7, **LAST).start()
    share_old(6)
    other_core(5)
    units(5, 6, 0, 3)
    share_old(7, **LAST)
    units(3, 6, 3, 4)
    other_core(6)
    other_core(7, **LAST)
    other_core(8, **OWN)
    units(6, 8, 0, 4)

    def finish(k, carry):
        sub = iota((REQS, ROWS), 0)
        slot = iota((REQS, ROWS), 1) & (SLOTS - 1)
        lse = peak_buf[k] + jnp.log(norm_buf[k])
        values = jnp.where(sub == slot, lse, jnp.where(sub == slot + SLOTS, pick_buf[k], 0.0))
        outbuf[...] += nt_dot(select_buf[k], values, EXACT)
        return carry

    lax.fori_loop(0, CHUNKS, finish, 0)

    def e1_copy(d):
        other = (group + d) % (NX * NC)
        return send(
            outbuf.at[pl.ds(pl.multiple_of(other * NZ, NZ), NZ)], in1.at[d], e1_s.at[d], e1_r.at[d],
            index_of(other // NC, z, other % NC), t,
        )

    for d in range(1, NX * NC):
        e1_copy(d).start()
    in1[0] = outbuf[pl.ds(pl.multiple_of(group * NZ, NZ), NZ), :]
    for d in range(1, NX * NC):
        e1_copy(d).wait_recv()

    def combine(values):
        peak = jnp.max(values, axis=0, keepdims=True)
        lse = peak + jnp.log(jnp.sum(jnp.exp(values - peak), axis=0, keepdims=True))
        pick = jnp.sum(values, axis=0, keepdims=True)
        return jnp.where(iota(lse.shape, 2) < SLOTS, lse, pick)[0]

    merged = combine(in1[...])
    for k in range(NZ):
        ex2[k] = merged[k : k + 1]

    def e2_copy(d):
        pz = (z + d) % NZ
        return send(ex2.at[pz], in2.at[d], e2_s.at[d], e2_r.at[d], index_of(x, pz, c), t)

    for d in range(1, NZ):
        e2_copy(d).start()
    in2[0] = ex2[z]
    for d in range(1, NZ):
        e2_copy(d).wait_recv()
    final = combine(in2[...])
    logprob = pltpu.roll(final, 128 - SLOTS, 1) - final
    lpbuf[...] = logprob
    in3[t] = logprob

    def e3_copy(d):
        return send(lpbuf, in3.at[t], e3_s.at[d], e3_r.at[d], req, (t + d) % NT)

    def e3_recv(d):
        return send(lpbuf, in3.at[(t + NT - d) % NT], e3_s.at[d], e3_r.at[d], req, (t + d) % NT)

    for d in range(1, NT):
        e3_copy(d).start()
    count = jnp.sum(jnp.where(owner[...] == req, lengths[...], 0), axis=1, keepdims=True)
    for d in range(1, NT):
        e3_recv(d).wait_recv()
    lane = iota((1, 128), 1)
    live0 = (lane < SLOTS) & (lane < count)
    live1 = (lane < SLOTS) & (lane + SLOTS < count)
    low, high = in3[0], in3[1]
    policy_total = jnp.sum(
        jnp.where(live0, low, 0.0) + jnp.where(live1, high, 0.0), axis=1, keepdims=True
    )
    ratio_total = jnp.sum(
        jnp.where(live0, low - in3[2], 0.0) + jnp.where(live1, high - in3[3], 0.0),
        axis=1, keepdims=True,
    )
    counts = count.astype(jnp.float32)
    scores = jnp.where(lane == 0, policy_total / counts, ratio_total / counts)
    scores_out[...] = scores[:, 0:2]
    mine = in3[t // 2]
    mine = jnp.where(half == 1, pltpu.roll(mine, 120, 1), mine)
    mine = jnp.where(lane + 8 * t < count, mine, 0.0)
    policy_out[...] = mine[:, 0:8]

    for d in range(1, NT):
        rs_copy(d).wait_send()
        tgt_copy(d).wait_send()
        e3_copy(d).wait_send()
    for d in range(1, NX):
        xa_copy(d).wait_send()
        xb_copy(8, d, **OWN).wait_send()
        xb_copy(7, d, **LAST).wait_send()
    twin_a(8, **OWN).wait_send()
    twin_b(8, **OWN).wait_send()
    twin_a(7, **LAST).wait_send()
    twin_b(7, **LAST).wait_send()

    def sent(n, carry):
        for d in range(1, NX):
            xb_copy(n, d).wait_send()
        twin_a(n).wait_send()
        twin_b(n).wait_send()
        return carry

    lax.fori_loop(0, 7, sent, 0)

    def head_sent(k, carry):
        pair_copy(k).wait_send()
        across_copy(k).wait_send()
        forward_copy(k).wait_send()
        return carry

    lax.fori_loop(0, PIECES, head_sent, 0)

    def ring_sent(side, s, first):
        for h in range(2):
            a_copy(side, s, h, first).wait_send()
        b_copy(side, s, first).wait_send()

    for side in range(2):
        ring_sent(side, 0, True)

        def side_sent(s, carry):
            ring_sent(side, s, False)
            return carry

        lax.fori_loop(1, 8 - side, side_sent, 0)
    for d in range(1, NX * NC):
        e1_copy(d).wait_send()
    for d in range(1, NZ):
        e2_copy(d).wait_send()


def per_device(
    queries,
    response_kv,
    cache_kv,
    residual,
    out_proj,
    norm_gain,
    lm_head,
    targets,
    resp_lengths,
    cache_lengths,
    owner_slot,
    sink_count,
    window_size,
):
    dma = pltpu.SemaphoreType.DMA
    vmem = pl.BlockSpec(memory_space=pltpu.VMEM)
    hbm = pl.BlockSpec(memory_space=pltpu.HBM)
    smem = pl.BlockSpec(memory_space=pltpu.SMEM)
    semaphores = [6] + [NT] * 4 + [PIECES] * 6 + [NX] * 2 + [16] * 4 + [8] * 4 + [36] * 2
    semaphores += [9] * 4 + [8] * 2 + [NZ] * 2 + [NT] * 2
    bf16, f32, i32 = jnp.bfloat16, jnp.float32, jnp.int32
    return pl.pallas_call(
        fused,
        out_shape=(jax.ShapeDtypeStruct((1, 8), f32), jax.ShapeDtypeStruct((1, 2), f32)),
        in_specs=[hbm] * 5 + [vmem, hbm] + [vmem] * 3 + [smem] * 3,
        out_specs=(vmem, vmem),
        scratch_shapes=[
            pltpu.VMEM((2, 1, RESP, FEAT), bf16),
            pltpu.VMEM((2, 2, KEYS, HEAD), bf16),
            pltpu.VMEM((2, FEAT, D), bf16),
            pltpu.VMEM((SLOTS, D), bf16),
            pltpu.VMEM((2, RESP, FEAT), bf16),
            pltpu.VMEM((2, RESP, D), f32),
            pltpu.VMEM((VOCAB_BLOCK, D), bf16),
            pltpu.VMEM((NX, CHUNKS, 2, NC, SLOTS, D), bf16),
            pltpu.VMEM((NT, SLOTS, D), f32),
            pltpu.VMEM((NT, NZ, ROWS), i32),
            pltpu.VMEM((NZ, ROWS), i32),
            pltpu.VMEM((NZ, ROWS), i32),
            pltpu.VMEM((CHUNKS, 1, ROWS), i32),
            pltpu.VMEM((CHUNKS, REQS, ROWS), f32),
            pltpu.VMEM((CHUNKS, 1, ROWS), f32),
            pltpu.VMEM((CHUNKS, 1, ROWS), f32),
            pltpu.VMEM((CHUNKS, 1, ROWS), f32),
            pltpu.VMEM((REQS, 128), f32),
            pltpu.VMEM((NX * NC, NZ, 128), f32),
            pltpu.VMEM((NZ, 1, 128), f32),
            pltpu.VMEM((NZ, 1, 128), f32),
            pltpu.VMEM((1, 128), f32),
            pltpu.VMEM((NT, 1, 128), f32),
        ]
        + [dma((n,)) for n in semaphores],
        compiler_params=pltpu.CompilerParams(
            collective_id=0, has_side_effects=True, vmem_limit_bytes=48 << 20
        ),
    )(
        queries,
        response_kv.reshape(2, 2, RESP, KV_HEADS * HEAD),
        cache_kv.reshape(2, 2, CACHE, KV_HEADS * HEAD),
        residual.reshape(2, RESP, D),
        out_proj,
        norm_gain,
        lm_head,
        targets,
        resp_lengths.reshape(1, REQS),
        owner_slot.reshape(1, REQS),
        cache_lengths,
        sink_count,
        window_size,
    )


def solution(mesh):
    in_specs = (
        P(None, "req", None, "tp"),
        P(None, "req", None, None, None),
        P(None, "req", None, None, None),
        P(None, "req", None, None),
        P(None, "tp", None),
        P(),
        P(None, "req", "tp"),
        P(None, "tp"),
        P(),
        P("req"),
        P(),
        P(),
        P(),
    )
    out_specs = (P("req", "tp"), P("req", None))
    return jax.shard_map(
        per_device, mesh=mesh, in_specs=in_specs, out_specs=out_specs, check_vma=False
    )
```

```python
import jax
import jax.numpy as jnp
from jax import lax
from jax.experimental import pallas as pl
from jax.experimental.pallas import tpu as pltpu
from jax.sharding import PartitionSpec as P

HEADS = 12
HEAD = 128
KV_HEADS = 2
RESP = 32
CACHE = 384
KEYS = CACHE + RESP
D = 1536

NX, NZ, NC, NT = 4, 16, 2, 4
REQS = NX * NZ * NC
SLOTS = 16
FEAT = D // NT
GROUP = HEADS // NT
VOCAB_BLOCK = 1024
PIECES = 4
PIECE = VOCAB_BLOCK // PIECES
CHUNKS = 8
ROWS = 2 * NX * NC * SLOTS
SPLIT = 128
MIDDLE = SPLIT + 768
A = pl.ds(0, SPLIT)
B = pl.ds(SPLIT, D - SPLIT)
B_PARTS = (pl.ds(SPLIT, MIDDLE - SPLIT), pl.ds(MIDDLE, D - MIDDLE))
OWN = 4 * 4 - 1
MESH = pl.DeviceIdType.MESH
EXACT = lax.Precision.HIGHEST


def iota(shape, dim):
    return lax.broadcasted_iota(jnp.int32, shape, dim)


def nt_dot(a, b, precision=None):
    return lax.dot_general(
        a, b, (((1,), (1,)), ((), ())), precision=precision, preferred_element_type=jnp.float32
    )


def fused(
    queries, response_kv, cache_kv, residual, out_proj, gain_in, head, targets_in, lengths_in,
    owner_in, cache_lengths_in, sink_count_in, window_size_in,
    policy_out, scores_out,
    gain, targets, lengths, owner, cache_lengths, sink_count, window_size,
    qbuf, kvbuf, wbuf, resbuf, attbuf, partial,
    hbuf, rows, rs_in, tgt_in, tgt_all, own_all, wanted_buf, select_buf,
    peak_buf, norm_buf, pick_buf, outbuf, in1, ex2, in2, in3,
    load_sem, rs_s, rs_r, tg_s, tg_r, hp_s, hp_r, hq_s, hq_r, hf_s, hf_r,
    xa_s, xa_r, za_s, za_r, zb_s, zb_r, xb_s, xb_r, c_s, c_r, e1_s, e1_r, e2_s, e2_r,
):
    req = lax.axis_index("req")
    t = lax.axis_index("tp")
    x = req // (NZ * NC)
    z = (req // NC) % NZ
    c = req % NC
    model = t // 2
    half = t % 2
    pair = t + 1 - 2 * (t % 2)
    across = NT - 1 - t
    group = x * NC + c

    def index_of(px, pz, pc):
        return (px * NZ + pz) * NC + pc

    def send(src, dst, ssem, rsem, preq, pt):
        return pltpu.make_async_remote_copy(
            src_ref=src, dst_ref=dst, send_sem=ssem, recv_sem=rsem,
            device_id={"req": preq, "tp": pt}, device_id_type=MESH,
        )

    def lanes(source):
        return pl.ds(pl.multiple_of(source * FEAT, FEAT), FEAT)

    barrier = pltpu.get_barrier_semaphore()

    def greet(preq, pt):
        pl.semaphore_signal(
            barrier, inc=1, device_id={"req": preq, "tp": pt}, device_id_type=MESH
        )

    for d in range(1, NX * NC):
        other = (group + d) % (NX * NC)
        greet(index_of(other // NC, z, other % NC), t)
    for d in range(1, NT):
        greet(req, (t + d) % NT)

    def greet_ring(d, carry):
        for e in range(NT):
            greet(index_of(x, (z + d) % NZ, c), (t + e) % NT)
        return carry

    lax.fori_loop(1, NZ, greet_ring, 0)

    kv_lanes = pl.ds(pl.multiple_of((t // 2) * HEAD, HEAD), HEAD)
    slot_start = pl.multiple_of(half * SLOTS, SLOTS)
    loads = [
        pltpu.make_async_copy(queries, qbuf, load_sem.at[0]),
        pltpu.make_async_copy(
            cache_kv.at[:, :, :, kv_lanes], kvbuf.at[:, :, pl.ds(0, CACHE)], load_sem.at[1]
        ),
        pltpu.make_async_copy(
            response_kv.at[:, :, :, kv_lanes], kvbuf.at[:, :, pl.ds(CACHE, RESP)], load_sem.at[2]
        ),
        pltpu.make_async_copy(out_proj, wbuf, load_sem.at[3]),
        pltpu.make_async_copy(residual.at[model, pl.ds(slot_start, SLOTS)], resbuf, load_sem.at[4]),
    ]
    small = [
        (cache_lengths_in, cache_lengths), (sink_count_in, sink_count),
        (window_size_in, window_size), (targets_in, targets), (owner_in, owner),
        (lengths_in, lengths), (gain_in, gain),
    ]
    small = [
        pltpu.make_async_copy(src, dst, load_sem.at[6 + i]) for i, (src, dst) in enumerate(small)
    ]
    own_head = pltpu.make_async_copy(head.at[model], hbuf.at[:, lanes(t)], load_sem.at[5])
    for copy in small + loads:
        copy.start()
    own_head.start()

    req_sub = iota((REQS, ROWS), 0)
    row_lane = iota((REQS, ROWS), 1)
    same_xc = ((req_sub >> 5) == (row_lane >> 6)) & ((req_sub & 1) == ((row_lane >> 4) & 1))
    same_z = ((iota((NZ, REQS), 1) >> 1) & (NZ - 1)) == iota((NZ, REQS), 0)
    zmask = jnp.where(same_z, 1.0, 0.0)

    pl.semaphore_wait(barrier, (NX * NC - 1) + (NT * NZ - 1))

    def piece(k):
        return pl.ds(k * PIECE, PIECE)

    def pair_copy(k):
        return send(
            head.at[model, piece(k)], hbuf.at[piece(k), lanes(t)], hp_s.at[k], hp_r.at[k], req, pair
        )

    def across_copy(k):
        return send(
            head.at[1 - model, piece(k)], hbuf.at[piece(k), lanes(t)], hq_s.at[k], hq_r.at[k],
            req, across,
        )

    def across_recv(k):
        return send(
            head.at[1 - model, piece(k)], hbuf.at[piece(k), lanes(across)], hq_s.at[k], hq_r.at[k],
            req, across,
        )

    def forward_copy(k):
        part = hbuf.at[piece(k), lanes(across)]
        return send(part, part, hf_s.at[k], hf_r.at[k], req, pair)

    def pair_recv(k):
        part = hbuf.at[piece(k), lanes(pair)]
        return send(part, part, hp_s.at[k], hp_r.at[k], req, pair)

    def forward_recv(k):
        part = hbuf.at[piece(k), lanes(NT - 1 - pair)]
        return send(part, part, hf_s.at[k], hf_r.at[k], req, pair)

    across_copy(0).start()
    pair_copy(0).start()
    across_copy(1).start()

    for copy in small + loads[:3]:
        copy.wait()
    length = cache_lengths[...]
    stack = (GROUP * RESP, KEYS)
    query_pos = length + (iota(stack, 0) & (RESP - 1))
    key = iota(stack, 1)
    key_pos = jnp.where(key < CACHE, key, length + key - CACHE)
    key_live = (key >= CACHE) | (key < length)
    inside = (key_pos < sink_count[...]) | (query_pos - key_pos < window_size[...])
    allowed = key_live & (key_pos <= query_pos) & inside
    for m in range(2):
        stacked = jnp.concatenate(
            [qbuf[m, 0, :, HEAD * g : HEAD * g + HEAD] for g in range(GROUP)], axis=0
        )
        scores = nt_dot(stacked, kvbuf[m, 0]) * HEAD ** (-0.5)
        masked = jnp.where(allowed, scores, -jnp.inf)
        weights = jnp.exp(masked - jnp.max(masked, axis=-1, keepdims=True))
        weights = (weights / jnp.sum(weights, axis=-1, keepdims=True)).astype(jnp.bfloat16)
        attended = jnp.dot(weights, kvbuf[m, 1], preferred_element_type=jnp.float32)
        attended = attended.astype(jnp.bfloat16)
        for g in range(GROUP):
            attbuf[m, :, HEAD * g : HEAD * g + HEAD] = attended[RESP * g : RESP * g + RESP]
    loads[3].wait()
    for m in range(2):
        partial[m] = jnp.dot(attbuf[m], wbuf[m], preferred_element_type=jnp.float32)

    def rs_copy(d):
        pt = (t + d) % NT
        start = pl.multiple_of((pt % 2) * SLOTS, SLOTS)
        return send(
            partial.at[pt // 2, pl.ds(start, SLOTS)], rs_in.at[d], rs_s.at[d], rs_r.at[d], req, pt
        )

    for d in range(1, NT):
        rs_copy(d).start()

    same_xc_wide = jnp.where(same_xc, 1.0, 0.0)
    wide = jnp.concatenate(
        [zmask * targets[s : s + 1, :].astype(jnp.float32) for s in range(8)], axis=0
    )
    wide = jnp.dot(wide, same_xc_wide, precision=EXACT, preferred_element_type=jnp.float32)
    slot_lane = iota((NZ, ROWS), 1) & (SLOTS - 1)
    placed = jnp.zeros((NZ, ROWS), jnp.float32)
    for s in range(8):
        placed = jnp.where(slot_lane == s + 8 * half, wide[NZ * s : NZ * s + NZ], placed)
    tgt_in[0] = placed.astype(jnp.int32)

    def tgt_copy(d):
        return send(tgt_in.at[0], tgt_in.at[d], tg_s.at[d], tg_r.at[d], req, (t + d) % NT)

    for d in range(1, NT):
        tgt_copy(d).start()
    own_all[...] = jnp.dot(
        zmask * owner[...].astype(jnp.float32), same_xc_wide, precision=EXACT,
        preferred_element_type=jnp.float32,
    ).astype(jnp.int32)

    def forward_head(k):
        across_recv(k).wait_recv()
        forward_copy(k).start()
        if k + 1 < PIECES:
            pair_copy(k + 1).start()

    across_copy(2).start()
    forward_head(0)
    across_copy(3).start()

    loads[4].wait()
    hidden = resbuf[...].astype(jnp.float32)
    total = partial[model, pl.ds(slot_start, SLOTS), :]
    for d in range(1, NT):
        rs_copy(d).wait_recv()
        total = total + rs_in[d]
    hidden = hidden + total
    scale_inv = lax.rsqrt(jnp.mean(hidden * hidden, axis=-1, keepdims=True) + 1e-06)
    rows[x, OWN, c] = (hidden * scale_inv * gain[pl.ds(model, 1), :]).astype(jnp.bfloat16)

    steps = range(1, 5)
    streams = [(side, j) for side in range(2) for j in range(2)]

    def slot_of(k, side, j):
        return 4 * (k - 1) + 2 * side + j

    def exists(k, side, j):
        return slot_of(k, side, j) != OWN

    def away(side, hops):
        return index_of(x, (z + hops) % NZ if side == 0 else (z + NZ - hops) % NZ, c)

    targets_of = [[away(side, 1), away(side, 2)] for side in range(2)]

    def z_copy(part_a, k, side, j):
        src = OWN if k == 1 else slot_of(k - 1, side, j)
        dst = slot_of(k, side, j)
        to = targets_of[side][j if k == 1 else 1]
        if part_a:
            return send(
                rows.at[:, src, c, :, A], rows.at[:, dst, c, :, A], za_s.at[dst], za_r.at[dst], to, t
            )
        return send(
            rows.at[x, src, c, :, B], rows.at[x, dst, c, :, B], zb_s.at[dst], zb_r.at[dst], to, t
        )

    beside = [index_of((x + d) % NX, z, c) for d in range(NX)]
    twin = index_of(x, z, 1 - c)

    def xa_copy(d):
        part = rows.at[x, OWN, c, :, A]
        return send(part, part, xa_s.at[d], xa_r.at[d], beside[d], t)

    def xa_recv(d):
        part = rows.at[(x + NX - d) % NX, OWN, c, :, A]
        return send(part, part, xa_s.at[d], xa_r.at[d], beside[d], t)

    groups = [(OWN, 1)] + [(4 * (k - 1) + 2 * side, 2) for k in steps for side in range(2)]
    groups[8] = (OWN - 1, 1)

    def x_part(g, block, part_lanes):
        start, size = groups[g]
        return rows.at[(x + block) % NX, pl.ds(start, size), c, :, part_lanes]

    def x_copy(g, way, second, receiving=False):
        back = NX - 1 if way == 0 else 1
        block = (back if second else 0) + (back if receiving else 0)
        part = x_part(g, block, B_PARTS[way] if second else B)
        n = 4 * g + 2 * second + way
        return send(part, part, xb_s.at[n], xb_r.at[n], beside[1 if way == 0 else NX - 1], t)

    def twin_copy(g, core):
        start, size = groups[g]
        part = rows.at[:, pl.ds(start, size), core]
        return send(part, part, c_s.at[g], c_r.at[g], twin, t)

    def x_send(g):
        for way in range(2):
            x_copy(g, way, 0).start()

    def x_pass(g):
        for way in range(2):
            x_copy(g, way, 0, True).wait_recv()
            x_copy(g, way, 1).start()

    def x_done(g):
        for way in range(2):
            x_copy(g, way, 1, True).wait_recv()
        twin_copy(g, c).start()

    def other_core(*gs):
        for g in gs:
            twin_copy(g, 1 - c).wait_recv()

    def arrive(k):
        for side in range(2):
            for j in range(2):
                if not exists(k, side, j):
                    continue
                for part_a in (True, False):
                    z_copy(part_a, k, side, j).wait_recv()
                    if k < 4 and exists(k + 1, side, j):
                        z_copy(part_a, k + 1, side, j).start()
            x_send(2 * k - 1 + side)

    for d in range(1, NX):
        xa_copy(d).start()
    for j in range(2):
        for side in range(2):
            z_copy(False, 1, side, j).start()
    x_send(0)
    for d in range(1, NX):
        xa_recv(d).wait_recv()
    for j in range(2):
        for side in range(2):
            z_copy(True, 1, side, j).start()
    forward_head(1)

    tgt_own = jnp.zeros((NZ, ROWS), jnp.int32)
    for d in range(NT):
        if d:
            tgt_copy(d).wait_recv()
        wanted_half = ((t + NT - d) % NT) // 2 == half
        tgt_own = tgt_own + jnp.where(wanted_half, tgt_in[d], 0)
    tgt_all[...] = tgt_own - req * VOCAB_BLOCK
    outbuf[...] = jnp.zeros_like(outbuf)
    peak_buf[...] = jnp.full_like(peak_buf, -jnp.inf)
    norm_buf[...] = jnp.zeros_like(norm_buf)
    pick_buf[...] = jnp.zeros_like(pick_buf)

    def prepare(n):
        if n % 2 == 0:
            z1, z2 = (z + NZ - n - 1) % NZ, (z + NZ - n - 2) % NZ
        else:
            z1, z2 = (z + n) % NZ, (z + (n + 1) % 8) % NZ
        first = (iota((1, ROWS), 1) & 32) == 0
        wanted_buf[n] = jnp.where(first, tgt_all[pl.ds(z1, 1), :], tgt_all[pl.ds(z2, 1), :])
        sub = iota((REQS, ROWS), 0)
        dest = ((sub >> 5) * NZ + (sub & (NZ - 1))) * NC + ((sub >> 4) & 1)
        place = jnp.where(first, own_all[pl.ds(z1, 1), :], own_all[pl.ds(z2, 1), :])
        select_buf[n] = jnp.where(dest == place, 1.0, 0.0).astype(jnp.bfloat16)

    def head_ready(k):
        pair_recv(k).wait_recv()
        forward_recv(k).wait_recv()

    def units(k0, k1, p0, p1):
        def unit(i, carry):
            k = k0 + i // (p1 - p0)
            p = p0 + i % (p1 - p0)
            base = pl.multiple_of(p * PIECE, PIECE)
            chunk = rows[:, pl.ds(2 * k, 2)].reshape(ROWS, D)
            logits = nt_dot(hbuf[pl.ds(base, PIECE), :], chunk)
            peak = jnp.max(logits, axis=0, keepdims=True)
            hit = iota((PIECE, ROWS), 0) == wanted_buf[k] - base
            pick_buf[k] += jnp.sum(jnp.where(hit, logits, 0.0), axis=0, keepdims=True)
            old = peak_buf[k]
            new = jnp.maximum(old, peak)
            norm = jnp.sum(jnp.exp(logits - new), axis=0, keepdims=True)
            norm_buf[k] = norm_buf[k] * jnp.exp(old - new) + norm
            peak_buf[k] = new
            return carry

        lax.fori_loop(0, (k1 - k0) * (p1 - p0), unit, 0)

    x_pass(0)
    arrive(1)
    forward_head(2)
    for n in range(4):
        prepare(n)
    x_done(0)

    x_pass(1)
    x_pass(2)
    arrive(2)
    forward_head(3)
    x_done(1)
    x_done(2)
    for n in range(4, CHUNKS):
        prepare(n)

    x_pass(3)
    x_pass(4)
    arrive(3)
    x_done(3)
    x_done(4)
    own_head.wait()
    head_ready(0)
    head_ready(1)
    other_core(1, 2)
    units(0, 2, 0, 2)

    x_pass(5)
    x_pass(6)
    arrive(4)
    x_done(5)
    x_done(6)
    other_core(3, 4)
    units(2, 4, 0, 2)
    x_pass(7)
    x_pass(8)
    head_ready(2)
    units(0, 4, 2, 3)
    head_ready(3)
    units(0, 4, 3, 4)
    other_core(5, 6)
    units(4, 6, 0, 2)
    x_done(7)
    x_done(8)
    units(4, 6, 2, 4)
    other_core(7, 8, 0)
    units(6, 8, 0, 4)

    def finish(k, carry):
        sub = iota((2 * SLOTS, ROWS), 0)
        slot = iota((2 * SLOTS, ROWS), 1) & (SLOTS - 1)
        lse = peak_buf[k] + jnp.log(norm_buf[k])
        values = jnp.where(sub == slot, lse, jnp.where(sub == slot + SLOTS, pick_buf[k], 0.0))
        terms = []
        for _ in range(3):
            terms.append(values.astype(jnp.bfloat16))
            values = values - terms[-1].astype(jnp.float32)
        terms.append(jnp.zeros_like(terms[0]))
        outbuf[...] += nt_dot(select_buf[k], jnp.concatenate(terms, axis=0))
        return carry

    lax.fori_loop(0, CHUNKS, finish, 0)
    found = outbuf[...]
    outbuf[...] = (found + pltpu.roll(found, 96, 1)) + pltpu.roll(found, 64, 1)

    def e1_copy(d):
        other = (group + d) % (NX * NC)
        return send(
            outbuf.at[pl.ds(pl.multiple_of(other * NZ, NZ), NZ)], in1.at[d], e1_s.at[d], e1_r.at[d],
            index_of(other // NC, z, other % NC), t,
        )

    for d in range(1, NX * NC):
        e1_copy(d).start()
    in1[0] = outbuf[pl.ds(pl.multiple_of(group * NZ, NZ), NZ), :]
    for d in range(1, NX * NC):
        e1_copy(d).wait_recv()

    def combine(values):
        peak = jnp.max(values, axis=0, keepdims=True)
        lse = peak + jnp.log(jnp.sum(jnp.exp(values - peak), axis=0, keepdims=True))
        pick = jnp.sum(values, axis=0, keepdims=True)
        return jnp.where(iota(lse.shape, 2) < SLOTS, lse, pick)[0]

    merged = combine(in1[...])
    for k in range(NZ):
        ex2[k] = merged[k : k + 1]

    def e2_copy(d, e):
        pz = (z + d) % NZ
        n = NT * d + e
        return send(
            ex2.at[pz], in2.at[t, d], e2_s.at[n], e2_r.at[n], index_of(x, pz, c), (t + e) % NT
        )

    def e2_recv(d, e):
        n = NT * d + e
        dst = in2.at[(t + NT - e) % NT, d]
        return send(ex2.at[0], dst, e2_s.at[n], e2_r.at[n], index_of(x, (z + d) % NZ, c), (t + e) % NT)

    def ring_loop(body):
        def step(d, carry):
            for e in range(NT):
                body(d, e)
            return carry

        for e in range(1, NT):
            body(0, e)
        lax.fori_loop(1, NZ, step, 0)

    ring_loop(lambda d, e: e2_copy(d, e).start())
    in2[t, 0] = ex2[z]
    count = jnp.sum(jnp.where(owner[...] == req, lengths[...], 0), axis=1, keepdims=True)
    ring_loop(lambda d, e: e2_recv(d, e).wait_recv())
    for column in range(NT):
        final = combine(in2[column])
        in3[column] = pltpu.roll(final, 128 - SLOTS, 1) - final
    lane = iota((1, 128), 1)
    live0 = (lane < SLOTS) & (lane < count)
    live1 = (lane < SLOTS) & (lane + SLOTS < count)
    low, high = in3[0], in3[1]
    policy_total = jnp.sum(
        jnp.where(live0, low, 0.0) + jnp.where(live1, high, 0.0), axis=1, keepdims=True
    )
    ratio_total = jnp.sum(
        jnp.where(live0, low - in3[2], 0.0) + jnp.where(live1, high - in3[3], 0.0),
        axis=1, keepdims=True,
    )
    counts = count.astype(jnp.float32)
    scores = jnp.where(lane == 0, policy_total / counts, ratio_total / counts)
    scores_out[...] = scores[:, 0:2]
    mine = in3[t // 2]
    mine = jnp.where(half == 1, pltpu.roll(mine, 120, 1), mine)
    mine = jnp.where(lane + 8 * t < count, mine, 0.0)
    policy_out[...] = mine[:, 0:8]

    for d in range(1, NT):
        rs_copy(d).wait_send()
        tgt_copy(d).wait_send()
    for d in range(1, NX):
        xa_copy(d).wait_send()
    for k in steps:
        for side, j in streams:
            if exists(k, side, j):
                z_copy(True, k, side, j).wait_send()
                z_copy(False, k, side, j).wait_send()
    for g in range(9):
        for way in range(2):
            x_copy(g, way, 0).wait_send()
            x_copy(g, way, 1).wait_send()
        twin_copy(g, c).wait_send()

    def head_sent(k, carry):
        pair_copy(k).wait_send()
        across_copy(k).wait_send()
        forward_copy(k).wait_send()
        return carry

    lax.fori_loop(0, PIECES, head_sent, 0)

    for d in range(1, NX * NC):
        e1_copy(d).wait_send()
    ring_loop(lambda d, e: e2_copy(d, e).wait_send())


def per_device(
    queries,
    response_kv,
    cache_kv,
    residual,
    out_proj,
    norm_gain,
    lm_head,
    targets,
    resp_lengths,
    cache_lengths,
    owner_slot,
    sink_count,
    window_size,
):
    dma = pltpu.SemaphoreType.DMA
    vmem = pl.BlockSpec(memory_space=pltpu.VMEM)
    hbm = pl.BlockSpec(memory_space=pltpu.HBM)
    semaphores = [13] + [NT] * 4 + [PIECES] * 6 + [NX] * 2 + [16] * 4 + [36] * 2
    semaphores += [9] * 2 + [8] * 2 + [NZ * NT] * 2
    bf16, f32, i32 = jnp.bfloat16, jnp.float32, jnp.int32
    return pl.pallas_call(
        fused,
        out_shape=(jax.ShapeDtypeStruct((1, 8), f32), jax.ShapeDtypeStruct((1, 2), f32)),
        in_specs=[hbm] * 13,
        out_specs=(vmem, vmem),
        scratch_shapes=[
            pltpu.VMEM((2, D), f32),
            pltpu.VMEM((RESP // NT, REQS), i32),
            pltpu.VMEM((1, REQS), i32),
            pltpu.VMEM((1, REQS), i32),
            pltpu.VMEM((1, 1), i32),
            pltpu.VMEM((1, 1), i32),
            pltpu.VMEM((1, 1), i32),
            pltpu.VMEM((2, 1, RESP, FEAT), bf16),
            pltpu.VMEM((2, 2, KEYS, HEAD), bf16),
            pltpu.VMEM((2, FEAT, D), bf16),
            pltpu.VMEM((SLOTS, D), bf16),
            pltpu.VMEM((2, RESP, FEAT), bf16),
            pltpu.VMEM((2, RESP, D), f32),
            pltpu.VMEM((VOCAB_BLOCK, D), bf16),
            pltpu.VMEM((NX, 2 * CHUNKS, NC, SLOTS, D), bf16),
            pltpu.VMEM((NT, SLOTS, D), f32),
            pltpu.VMEM((NT, NZ, ROWS), i32),
            pltpu.VMEM((NZ, ROWS), i32),
            pltpu.VMEM((NZ, ROWS), i32),
            pltpu.VMEM((CHUNKS, 1, ROWS), i32),
            pltpu.VMEM((CHUNKS, REQS, ROWS), bf16),
            pltpu.VMEM((CHUNKS, 1, ROWS), f32),
            pltpu.VMEM((CHUNKS, 1, ROWS), f32),
            pltpu.VMEM((CHUNKS, 1, ROWS), f32),
            pltpu.VMEM((REQS, 128), f32),
            pltpu.VMEM((NX * NC, NZ, 128), f32),
            pltpu.VMEM((NZ, 1, 128), f32),
            pltpu.VMEM((NT, NZ, 1, 128), f32),
            pltpu.VMEM((NT, 1, 128), f32),
        ]
        + [dma((n,)) for n in semaphores],
        compiler_params=pltpu.CompilerParams(
            collective_id=0, has_side_effects=True, vmem_limit_bytes=63 << 20
        ),
    )(
        queries,
        response_kv.reshape(2, 2, RESP, KV_HEADS * HEAD),
        cache_kv.reshape(2, 2, CACHE, KV_HEADS * HEAD),
        residual.reshape(2, RESP, D),
        out_proj,
        norm_gain,
        lm_head,
        targets.T,
        resp_lengths.reshape(1, REQS),
        owner_slot.reshape(1, REQS),
        cache_lengths.reshape(1, 1),
        sink_count.reshape(1, 1),
        window_size.reshape(1, 1),
    )


def solution(mesh):
    in_specs = (
        P(None, "req", None, "tp"),
        P(None, "req", None, None, None),
        P(None, "req", None, None, None),
        P(None, "req", None, None),
        P(None, "tp", None),
        P(),
        P(None, "req", "tp"),
        P(None, "tp"),
        P(),
        P("req"),
        P(),
        P(),
        P(),
    )
    out_specs = (P("req", "tp"), P("req", None))
    return jax.shard_map(
        per_device, mesh=mesh, in_specs=in_specs, out_specs=out_specs, check_vma=False
    )
```

```python
import jax
import jax.numpy as jnp
from jax import lax
from jax.experimental import pallas as pl
from jax.experimental.pallas import tpu as pltpu
from jax.sharding import PartitionSpec as P

HEADS = 12
HEAD = 128
KV_HEADS = 2
RESP = 32
CACHE = 384
KEYS = CACHE + RESP
D = 1536

NX, NZ, NC, NT = 4, 16, 2, 4
REQS = NX * NZ * NC
SLOTS = 16
FEAT = D // NT
GROUP = HEADS // NT
VOCAB_BLOCK = 1024
PIECES = 4
PIECE = VOCAB_BLOCK // PIECES
CHUNKS = 4
ROWS = 4 * NX * NC * SLOTS
BLOCK = 512
FEATURE_HALVES = (pl.ds(0, D // 2), pl.ds(D // 2, D // 2))
ALL = pl.ds(0, D)
OWN = 4 * 4 - 1
MESH = pl.DeviceIdType.MESH
EXACT = lax.Precision.HIGHEST


def iota(shape, dim):
    return lax.broadcasted_iota(jnp.int32, shape, dim)


def nt_dot(a, b, precision=None):
    return lax.dot_general(
        a, b, (((1,), (1,)), ((), ())), precision=precision, preferred_element_type=jnp.float32
    )


def fused(
    queries, response_kv, cache_kv, residual, out_proj, gain_in, head, targets_in, lengths_in,
    owner_in, cache_lengths_in, sink_count_in, window_size_in,
    policy_out, scores_out,
    gain, targets, lengths, owner, cache_lengths, sink_count, window_size,
    qbuf, kvbuf, wbuf, resbuf, attbuf, partial,
    hbuf, rows, rs_in, tgt_in, tgt_all, own_all, wanted_buf, select_buf,
    peak_buf, norm_buf, pick_buf, outbuf, in1, ex2, in2, in3,
    load_sem, rs_s, rs_r, tg_s, tg_r, hp_s, hp_r, hq_s, hq_r, hf_s, hf_r,
    z_s, z_r, x_s, x_r, c_s, c_r, e1_s, e1_r, e2_s, e2_r,
):
    req = lax.axis_index("req")
    t = lax.axis_index("tp")
    x = req // (NZ * NC)
    z = (req // NC) % NZ
    c = req % NC
    model = t // 2
    half = t % 2
    pair = t + 1 - 2 * (t % 2)
    across = NT - 1 - t
    group = x * NC + c

    def index_of(px, pz, pc):
        return (px * NZ + pz) * NC + pc

    def send(src, dst, ssem, rsem, preq, pt):
        return pltpu.make_async_remote_copy(
            src_ref=src, dst_ref=dst, send_sem=ssem, recv_sem=rsem,
            device_id={"req": preq, "tp": pt}, device_id_type=MESH,
        )

    def lanes(source):
        return pl.ds(pl.multiple_of(source * FEAT, FEAT), FEAT)

    barrier = pltpu.get_barrier_semaphore()

    def greet(preq, pt):
        pl.semaphore_signal(
            barrier, inc=1, device_id={"req": preq, "tp": pt}, device_id_type=MESH
        )

    for d in range(1, NX * NC):
        other = (group + d) % (NX * NC)
        greet(index_of(other // NC, z, other % NC), t)
    for d in range(1, NT):
        greet(req, (t + d) % NT)

    def greet_ring(d, carry):
        for e in range(NT):
            greet(index_of(x, (z + d) % NZ, c), (t + e) % NT)
        return carry

    lax.fori_loop(1, NZ, greet_ring, 0)

    kv_lanes = pl.ds(pl.multiple_of((t // 2) * HEAD, HEAD), HEAD)
    slot_start = pl.multiple_of(half * SLOTS, SLOTS)
    loads = [
        pltpu.make_async_copy(queries, qbuf, load_sem.at[0]),
        pltpu.make_async_copy(
            cache_kv.at[:, :, :, kv_lanes], kvbuf.at[:, :, pl.ds(0, CACHE)], load_sem.at[1]
        ),
        pltpu.make_async_copy(
            response_kv.at[:, :, :, kv_lanes], kvbuf.at[:, :, pl.ds(CACHE, RESP)], load_sem.at[2]
        ),
        pltpu.make_async_copy(out_proj, wbuf, load_sem.at[3]),
        pltpu.make_async_copy(residual.at[model, pl.ds(slot_start, SLOTS)], resbuf, load_sem.at[4]),
    ]
    small = [
        (cache_lengths_in, cache_lengths), (sink_count_in, sink_count),
        (window_size_in, window_size), (targets_in, targets), (owner_in, owner),
        (lengths_in, lengths), (gain_in, gain),
    ]
    small = [
        pltpu.make_async_copy(src, dst, load_sem.at[6 + i]) for i, (src, dst) in enumerate(small)
    ]
    own_head = pltpu.make_async_copy(head.at[model], hbuf.at[:, lanes(t)], load_sem.at[5])
    for copy in small + loads:
        copy.start()
    own_head.start()

    req_sub = iota((REQS, ROWS), 0)
    row_lane = iota((REQS, ROWS), 1)
    same_xc = ((req_sub >> 5) == (row_lane >> 7)) & ((req_sub & 1) == ((row_lane >> 4) & 1))
    same_z = ((iota((NZ, REQS), 1) >> 1) & (NZ - 1)) == iota((NZ, REQS), 0)
    zmask = jnp.where(same_z, 1.0, 0.0)

    pl.semaphore_wait(barrier, (NX * NC - 1) + (NT * NZ - 1))

    def piece(k):
        return pl.ds(k * PIECE, PIECE)

    def pair_copy(k):
        return send(
            head.at[model, piece(k)], hbuf.at[piece(k), lanes(t)], hp_s.at[k], hp_r.at[k], req, pair
        )

    def across_copy(k):
        return send(
            head.at[1 - model, piece(k)], hbuf.at[piece(k), lanes(t)], hq_s.at[k], hq_r.at[k],
            req, across,
        )

    def across_recv(k):
        return send(
            head.at[1 - model, piece(k)], hbuf.at[piece(k), lanes(across)], hq_s.at[k], hq_r.at[k],
            req, across,
        )

    def forward_copy(k):
        part = hbuf.at[piece(k), lanes(across)]
        return send(part, part, hf_s.at[k], hf_r.at[k], req, pair)

    def pair_recv(k):
        part = hbuf.at[piece(k), lanes(pair)]
        return send(part, part, hp_s.at[k], hp_r.at[k], req, pair)

    def forward_recv(k):
        part = hbuf.at[piece(k), lanes(NT - 1 - pair)]
        return send(part, part, hf_s.at[k], hf_r.at[k], req, pair)

    across_copy(0).start()
    pair_copy(0).start()
    across_copy(1).start()

    for copy in small + loads[:3]:
        copy.wait()
    length = cache_lengths[...]
    stack = (GROUP * RESP, KEYS)
    query_pos = length + (iota(stack, 0) & (RESP - 1))
    key = iota(stack, 1)
    key_pos = jnp.where(key < CACHE, key, length + key - CACHE)
    key_live = (key >= CACHE) | (key < length)
    inside = (key_pos < sink_count[...]) | (query_pos - key_pos < window_size[...])
    allowed = key_live & (key_pos <= query_pos) & inside
    for m in range(2):
        stacked = jnp.concatenate(
            [qbuf[m, 0, :, HEAD * g : HEAD * g + HEAD] for g in range(GROUP)], axis=0
        )
        scores = nt_dot(stacked, kvbuf[m, 0]) * HEAD ** (-0.5)
        masked = jnp.where(allowed, scores, -jnp.inf)
        weights = jnp.exp(masked - jnp.max(masked, axis=-1, keepdims=True))
        weights = (weights / jnp.sum(weights, axis=-1, keepdims=True)).astype(jnp.bfloat16)
        attended = jnp.dot(weights, kvbuf[m, 1], preferred_element_type=jnp.float32)
        attended = attended.astype(jnp.bfloat16)
        for g in range(GROUP):
            attbuf[m, :, HEAD * g : HEAD * g + HEAD] = attended[RESP * g : RESP * g + RESP]
    loads[3].wait()
    for m in range(2):
        partial[m] = jnp.dot(attbuf[m], wbuf[m], preferred_element_type=jnp.float32)

    def rs_copy(d):
        pt = (t + d) % NT
        start = pl.multiple_of((pt % 2) * SLOTS, SLOTS)
        return send(
            partial.at[pt // 2, pl.ds(start, SLOTS)], rs_in.at[d], rs_s.at[d], rs_r.at[d], req, pt
        )

    for d in range(1, NT):
        rs_copy(d).start()

    lane128 = iota((REQS, 128), 1)
    sub128 = iota((REQS, 128), 0)
    same_xc_lane = ((sub128 >> 5) == (lane128 >> 5)) & ((sub128 & 1) == ((lane128 >> 4) & 1))
    wide = jnp.concatenate(
        [zmask * targets[s : s + 1, :].astype(jnp.float32) for s in range(8)], axis=0
    )
    wide = jnp.dot(
        wide, jnp.where(same_xc_lane, 1.0, 0.0), precision=EXACT,
        preferred_element_type=jnp.float32,
    )
    slot_lane = iota((NZ, 128), 1) & (SLOTS - 1)
    placed = jnp.zeros((NZ, 128), jnp.float32)
    for s in range(8):
        placed = jnp.where(slot_lane == s + 8 * half, wide[NZ * s : NZ * s + NZ], placed)
    tgt_in[0] = placed.astype(jnp.int32)

    def tgt_copy(d):
        return send(tgt_in.at[0], tgt_in.at[d], tg_s.at[d], tg_r.at[d], req, (t + d) % NT)

    for d in range(1, NT):
        tgt_copy(d).start()
    own_all[...] = jnp.dot(
        zmask * owner[...].astype(jnp.float32), jnp.where(same_xc, 1.0, 0.0), precision=EXACT,
        preferred_element_type=jnp.float32,
    ).astype(jnp.int32)

    def forward_head(k):
        across_recv(k).wait_recv()
        forward_copy(k).start()
        if k in (1, 2):
            pair_copy(k + 1).start()

    pair_copy(1).start()
    across_copy(2).start()
    forward_head(0)
    across_copy(3).start()

    loads[4].wait()
    hidden = resbuf[...].astype(jnp.float32)
    total = partial[model, pl.ds(slot_start, SLOTS), :]
    for d in range(1, NT):
        rs_copy(d).wait_recv()
        total = total + rs_in[d]
    hidden = hidden + total
    scale_inv = lax.rsqrt(jnp.mean(hidden * hidden, axis=-1, keepdims=True) + 1e-06)
    rows[x, OWN, c] = (hidden * scale_inv * gain[pl.ds(model, 1), :]).astype(jnp.bfloat16)

    steps = range(1, 5)
    streams = [(side, j) for side in range(2) for j in range(2)]

    def slot_of(k, side, j):
        return 4 * (k - 1) + 2 * side + j

    def exists(k, side, j):
        return slot_of(k, side, j) != OWN

    def away(side, hops):
        return index_of(x, (z + hops) % NZ if side == 0 else (z + NZ - hops) % NZ, c)

    targets_of = [[away(side, 1), away(side, 2)] for side in range(2)]

    def z_copy(k, side, j):
        src = OWN if k == 1 else slot_of(k - 1, side, j)
        dst = slot_of(k, side, j)
        to = targets_of[side][j if k == 1 else 1]
        return send(rows.at[x, src, c], rows.at[x, dst, c], z_s.at[dst], z_r.at[dst], to, t)

    beside = [index_of((x + d) % NX, z, c) for d in range(NX)]
    twin = index_of(x, z, 1 - c)

    groups = [(OWN, 1)] + [(4 * (k - 1) + 2 * side, 2) for k in steps for side in range(2)]
    groups[8] = (OWN - 1, 1)

    def x_part(g, block, part_lanes):
        start, size = groups[g]
        return rows.at[(x + block) % NX, pl.ds(start, size), c, :, part_lanes]

    def x_copy(g, way, second, receiving=False):
        back = NX - 1 if way == 0 else 1
        block = (back if second else 0) + (back if receiving else 0)
        part = x_part(g, block, FEATURE_HALVES[way] if second else ALL)
        n = 4 * g + 2 * second + way
        return send(part, part, x_s.at[n], x_r.at[n], beside[1 if way == 0 else NX - 1], t)

    def twin_copy(g, core):
        start, size = groups[g]
        part = rows.at[:, pl.ds(start, size), core]
        return send(part, part, c_s.at[g], c_r.at[g], twin, t)

    def x_send(g):
        for way in range(2):
            x_copy(g, way, 0).start()

    def x_pass(g):
        for way in range(2):
            x_copy(g, way, 0, True).wait_recv()
            x_copy(g, way, 1).start()

    def x_done(g):
        for way in range(2):
            x_copy(g, way, 1, True).wait_recv()
        twin_copy(g, c).start()

    def other_core(*gs):
        for g in gs:
            twin_copy(g, 1 - c).wait_recv()

    def arrive(k):
        for side in range(2):
            for j in range(2):
                if not exists(k, side, j):
                    continue
                z_copy(k, side, j).wait_recv()
                if k < 4 and exists(k + 1, side, j):
                    z_copy(k + 1, side, j).start()
            x_send(2 * k - 1 + side)

    for j in range(2):
        for side in range(2):
            z_copy(1, side, j).start()
    x_send(0)
    forward_head(1)

    tgt_own = jnp.zeros((NZ, 128), jnp.int32)
    for d in range(NT):
        if d:
            tgt_copy(d).wait_recv()
        wanted_half = ((t + NT - d) % NT) // 2 == half
        tgt_own = tgt_own + jnp.where(wanted_half, tgt_in[d], 0)
    small_lane = ((iota((128, ROWS), 1) >> 7) << 5) + (iota((128, ROWS), 1) & 31)
    repeat = jnp.where(small_lane == iota((128, ROWS), 0), 1.0, 0.0)
    tgt_wide = jnp.dot(
        tgt_own.astype(jnp.float32), repeat, precision=EXACT, preferred_element_type=jnp.float32
    )
    tgt_all[...] = tgt_wide.astype(jnp.int32) - req * VOCAB_BLOCK
    outbuf[...] = jnp.zeros_like(outbuf)
    peak_buf[...] = jnp.full_like(peak_buf, -jnp.inf)
    norm_buf[...] = jnp.zeros_like(norm_buf)
    pick_buf[...] = jnp.zeros_like(pick_buf)

    def prepare(k):
        near, far = 2 * k + 1, 2 * k + 2
        places = [(z + NZ - near) % NZ, (z + NZ - far) % NZ, (z + near) % NZ, (z + far % 8) % NZ]
        place = (iota((1, ROWS), 1) >> 5) & 3

        def pick(table):
            found = table[pl.ds(places[3], 1), :]
            for i in range(3):
                found = jnp.where(place == i, table[pl.ds(places[i], 1), :], found)
            return found

        wanted_buf[k] = pick(tgt_all)
        sub = iota((REQS, ROWS), 0)
        dest = ((sub >> 5) * NZ + (sub & (NZ - 1))) * NC + ((sub >> 4) & 1)
        select_buf[k] = jnp.where(dest == pick(own_all), 1.0, 0.0).astype(jnp.bfloat16)

    def head_ready(k):
        pair_recv(k).wait_recv()
        forward_recv(k).wait_recv()

    def units(k0, k1, p0, p1):
        def unit(i, carry):
            k = k0 + i // (p1 - p0)
            p = p0 + i % (p1 - p0)
            base = pl.multiple_of(p * BLOCK, BLOCK)
            chunk = rows[:, pl.ds(4 * k, 4)].reshape(ROWS, D)
            logits = nt_dot(hbuf[pl.ds(base, BLOCK), :], chunk)
            peak = jnp.max(logits, axis=0, keepdims=True)
            hit = iota((BLOCK, ROWS), 0) == wanted_buf[k] - base
            pick_buf[k] += jnp.sum(jnp.where(hit, logits, 0.0), axis=0, keepdims=True)
            old = peak_buf[k]
            new = jnp.maximum(old, peak)
            norm = jnp.sum(jnp.exp(logits - new), axis=0, keepdims=True)
            norm_buf[k] = norm_buf[k] * jnp.exp(old - new) + norm
            peak_buf[k] = new
            return carry

        lax.fori_loop(0, (k1 - k0) * (p1 - p0), unit, 0)

    x_pass(0)
    arrive(1)
    forward_head(2)
    prepare(0)
    prepare(1)
    x_done(0)

    x_pass(1)
    x_pass(2)
    arrive(2)
    forward_head(3)
    x_done(1)
    x_done(2)
    prepare(2)
    prepare(3)

    x_pass(3)
    x_pass(4)
    arrive(3)
    x_done(3)
    x_done(4)
    own_head.wait()
    head_ready(0)
    head_ready(1)
    other_core(1, 2)
    units(0, 1, 0, 1)

    x_pass(5)
    x_pass(6)
    arrive(4)
    x_done(5)
    x_done(6)
    other_core(3, 4)
    units(1, 2, 0, 1)
    x_pass(7)
    x_pass(8)
    other_core(5, 6)
    units(2, 3, 0, 1)
    head_ready(2)
    head_ready(3)
    units(0, 2, 1, 2)
    x_done(7)
    x_done(8)
    units(2, 3, 1, 2)
    other_core(7, 8, 0)
    units(3, 4, 0, 2)

    def finish(k, carry):
        sub = iota((2 * SLOTS, ROWS), 0)
        slot = iota((2 * SLOTS, ROWS), 1) & (SLOTS - 1)
        lse = peak_buf[k] + jnp.log(norm_buf[k])
        values = jnp.where(sub == slot, lse, jnp.where(sub == slot + SLOTS, pick_buf[k], 0.0))
        terms = []
        for _ in range(3):
            terms.append(values.astype(jnp.bfloat16))
            values = values - terms[-1].astype(jnp.float32)
        terms.append(jnp.zeros_like(terms[0]))
        outbuf[...] += nt_dot(select_buf[k], jnp.concatenate(terms, axis=0))
        return carry

    lax.fori_loop(0, CHUNKS, finish, 0)
    found = outbuf[...]
    outbuf[...] = (found + pltpu.roll(found, 96, 1)) + pltpu.roll(found, 64, 1)

    def e1_copy(d):
        other = (group + d) % (NX * NC)
        return send(
            outbuf.at[pl.ds(pl.multiple_of(other * NZ, NZ), NZ)], in1.at[d], e1_s.at[d], e1_r.at[d],
            index_of(other // NC, z, other % NC), t,
        )

    for d in range(1, NX * NC):
        e1_copy(d).start()
    in1[0] = outbuf[pl.ds(pl.multiple_of(group * NZ, NZ), NZ), :]
    for d in range(1, NX * NC):
        e1_copy(d).wait_recv()

    def combine(values):
        peak = jnp.max(values, axis=0, keepdims=True)
        lse = peak + jnp.log(jnp.sum(jnp.exp(values - peak), axis=0, keepdims=True))
        pick = jnp.sum(values, axis=0, keepdims=True)
        return jnp.where(iota(lse.shape, 2) < SLOTS, lse, pick)[0]

    merged = combine(in1[...])
    for k in range(NZ):
        ex2[k] = merged[k : k + 1]

    def e2_copy(d, e):
        pz = (z + d) % NZ
        n = NT * d + e
        return send(
            ex2.at[pz], in2.at[t, d], e2_s.at[n], e2_r.at[n], index_of(x, pz, c), (t + e) % NT
        )

    def e2_recv(d, e):
        n = NT * d + e
        dst = in2.at[(t + NT - e) % NT, d]
        return send(ex2.at[0], dst, e2_s.at[n], e2_r.at[n], index_of(x, (z + d) % NZ, c), (t + e) % NT)

    def ring_loop(body):
        def step(d, carry):
            for e in range(NT):
                body(d, e)
            return carry

        for e in range(1, NT):
            body(0, e)
        lax.fori_loop(1, NZ, step, 0)

    ring_loop(lambda d, e: e2_copy(d, e).start())
    in2[t, 0] = ex2[z]
    count = jnp.sum(jnp.where(owner[...] == req, lengths[...], 0), axis=1, keepdims=True)
    ring_loop(lambda d, e: e2_recv(d, e).wait_recv())
    for column in range(NT):
        final = combine(in2[column])
        in3[column] = pltpu.roll(final, 128 - SLOTS, 1) - final
    lane = iota((1, 128), 1)
    live0 = (lane < SLOTS) & (lane < count)
    live1 = (lane < SLOTS) & (lane + SLOTS < count)
    low, high = in3[0], in3[1]
    policy_total = jnp.sum(
        jnp.where(live0, low, 0.0) + jnp.where(live1, high, 0.0), axis=1, keepdims=True
    )
    ratio_total = jnp.sum(
        jnp.where(live0, low - in3[2], 0.0) + jnp.where(live1, high - in3[3], 0.0),
        axis=1, keepdims=True,
    )
    counts = count.astype(jnp.float32)
    scores = jnp.where(lane == 0, policy_total / counts, ratio_total / counts)
    scores_out[...] = scores[:, 0:2]
    mine = in3[t // 2]
    mine = jnp.where(half == 1, pltpu.roll(mine, 120, 1), mine)
    mine = jnp.where(lane + 8 * t < count, mine, 0.0)
    policy_out[...] = mine[:, 0:8]

    for d in range(1, NT):
        rs_copy(d).wait_send()
        tgt_copy(d).wait_send()
    for k in steps:
        for side, j in streams:
            if exists(k, side, j):
                z_copy(k, side, j).wait_send()
    for g in range(9):
        for way in range(2):
            x_copy(g, way, 0).wait_send()
            x_copy(g, way, 1).wait_send()
        twin_copy(g, c).wait_send()

    def head_sent(k, carry):
        pair_copy(k).wait_send()
        across_copy(k).wait_send()
        forward_copy(k).wait_send()
        return carry

    lax.fori_loop(0, PIECES, head_sent, 0)

    for d in range(1, NX * NC):
        e1_copy(d).wait_send()
    ring_loop(lambda d, e: e2_copy(d, e).wait_send())


def per_device(
    queries,
    response_kv,
    cache_kv,
    residual,
    out_proj,
    norm_gain,
    lm_head,
    targets,
    resp_lengths,
    cache_lengths,
    owner_slot,
    sink_count,
    window_size,
):
    dma = pltpu.SemaphoreType.DMA
    vmem = pl.BlockSpec(memory_space=pltpu.VMEM)
    hbm = pl.BlockSpec(memory_space=pltpu.HBM)
    semaphores = [13] + [NT] * 4 + [PIECES] * 6 + [16] * 2 + [36] * 2
    semaphores += [9] * 2 + [8] * 2 + [NZ * NT] * 2
    bf16, f32, i32 = jnp.bfloat16, jnp.float32, jnp.int32
    return pl.pallas_call(
        fused,
        out_shape=(jax.ShapeDtypeStruct((1, 8), f32), jax.ShapeDtypeStruct((1, 2), f32)),
        in_specs=[hbm] * 13,
        out_specs=(vmem, vmem),
        scratch_shapes=[
            pltpu.VMEM((2, D), f32),
            pltpu.VMEM((RESP // NT, REQS), i32),
            pltpu.VMEM((1, REQS), i32),
            pltpu.VMEM((1, REQS), i32),
            pltpu.VMEM((1, 1), i32),
            pltpu.VMEM((1, 1), i32),
            pltpu.VMEM((1, 1), i32),
            pltpu.VMEM((2, 1, RESP, FEAT), bf16),
            pltpu.VMEM((2, 2, KEYS, HEAD), bf16),
            pltpu.VMEM((2, FEAT, D), bf16),
            pltpu.VMEM((SLOTS, D), bf16),
            pltpu.VMEM((2, RESP, FEAT), bf16),
            pltpu.VMEM((2, RESP, D), f32),
            pltpu.VMEM((VOCAB_BLOCK, D), bf16),
            pltpu.VMEM((NX, NZ, NC, SLOTS, D), bf16),
            pltpu.VMEM((NT, SLOTS, D), f32),
            pltpu.VMEM((NT, NZ, 128), i32),
            pltpu.VMEM((NZ, ROWS), i32),
            pltpu.VMEM((NZ, ROWS), i32),
            pltpu.VMEM((CHUNKS, 1, ROWS), i32),
            pltpu.VMEM((CHUNKS, REQS, ROWS), bf16),
            pltpu.VMEM((CHUNKS, 1, ROWS), f32),
            pltpu.VMEM((CHUNKS, 1, ROWS), f32),
            pltpu.VMEM((CHUNKS, 1, ROWS), f32),
            pltpu.VMEM((REQS, 128), f32),
            pltpu.VMEM((NX * NC, NZ, 128), f32),
            pltpu.VMEM((NZ, 1, 128), f32),
            pltpu.VMEM((NT, NZ, 1, 128), f32),
            pltpu.VMEM((NT, 1, 128), f32),
        ]
        + [dma((n,)) for n in semaphores],
        compiler_params=pltpu.CompilerParams(
            collective_id=0, has_side_effects=True, vmem_limit_bytes=63 << 20
        ),
    )(
        queries,
        response_kv.reshape(2, 2, RESP, KV_HEADS * HEAD),
        cache_kv.reshape(2, 2, CACHE, KV_HEADS * HEAD),
        residual.reshape(2, RESP, D),
        out_proj,
        norm_gain,
        lm_head,
        targets.T,
        resp_lengths.reshape(1, REQS),
        owner_slot.reshape(1, REQS),
        cache_lengths.reshape(1, 1),
        sink_count.reshape(1, 1),
        window_size.reshape(1, 1),
    )


def solution(mesh):
    in_specs = (
        P(None, "req", None, "tp"),
        P(None, "req", None, None, None),
        P(None, "req", None, None, None),
        P(None, "req", None, None),
        P(None, "tp", None),
        P(),
        P(None, "req", "tp"),
        P(None, "tp"),
        P(),
        P("req"),
        P(),
        P(),
        P(),
    )
    out_specs = (P("req", "tp"), P("req", None))
    return jax.shard_map(
        per_device, mesh=mesh, in_specs=in_specs, out_specs=out_specs, check_vma=False
    )
```

```python
import jax
import jax.numpy as jnp
from jax import lax
from jax.experimental import pallas as pl
from jax.experimental.pallas import tpu as pltpu
from jax.sharding import PartitionSpec as P

HEADS = 12
HEAD = 128
KV_HEADS = 2
RESP = 32
CACHE = 384
KEYS = CACHE + RESP
D = 1536

NX, NZ, NC, NT = 4, 16, 2, 4
REQS = NX * NZ * NC
SLOTS = 16
FEAT = D // NT
GROUP = HEADS // NT
VOCAB_BLOCK = 1024
PIECES = 4
PIECE = VOCAB_BLOCK // PIECES
CHUNKS = 4
ROWS = 4 * NX * NC * SLOTS
BLOCK = 512
FEATURE_HALVES = (pl.ds(0, D // 2), pl.ds(D // 2, D // 2))
ALL = pl.ds(0, D)
OWN = 4 * 4 - 1
MESH = pl.DeviceIdType.MESH
EXACT = lax.Precision.HIGHEST


def iota(shape, dim):
    return lax.broadcasted_iota(jnp.int32, shape, dim)


def nt_dot(a, b, precision=None):
    return lax.dot_general(
        a, b, (((1,), (1,)), ((), ())), precision=precision, preferred_element_type=jnp.float32
    )


def fused(
    queries, response_kv, cache_kv, residual, out_proj, gain_in, head, targets_in, lengths_in,
    owner_in, cache_lengths_in, sink_count_in, window_size_in,
    policy_out, scores_out,
    gain, targets, lengths, owner, cache_lengths, sink_count, window_size,
    qbuf, kvbuf, wbuf, resbuf, attbuf, partial,
    hbuf, rows, rs_in, tgt_in, tgt_all, own_all, wanted_buf, select_buf,
    peak_buf, norm_buf, pick_buf, outbuf, in1, ex2, in2, in3,
    load_sem, rs_s, rs_r, tg_s, tg_r, hp_s, hp_r, hq_s, hq_r, hf_s, hf_r,
    z_s, z_r, x_s, x_r, c_s, c_r, e1_s, e1_r, e2_s, e2_r,
):
    req = lax.axis_index("req")
    t = lax.axis_index("tp")
    x = req // (NZ * NC)
    z = (req // NC) % NZ
    c = req % NC
    model = t // 2
    half = t % 2
    pair = t + 1 - 2 * (t % 2)
    across = NT - 1 - t
    group = x * NC + c

    def index_of(px, pz, pc):
        return (px * NZ + pz) * NC + pc

    def send(src, dst, ssem, rsem, preq, pt):
        return pltpu.make_async_remote_copy(
            src_ref=src, dst_ref=dst, send_sem=ssem, recv_sem=rsem,
            device_id={"req": preq, "tp": pt}, device_id_type=MESH,
        )

    def lanes(source):
        return pl.ds(pl.multiple_of(source * FEAT, FEAT), FEAT)

    barrier = pltpu.get_barrier_semaphore()

    def greet(preq, pt):
        pl.semaphore_signal(
            barrier, inc=1, device_id={"req": preq, "tp": pt}, device_id_type=MESH
        )

    for d in range(1, NX * NC):
        other = (group + d) % (NX * NC)
        greet(index_of(other // NC, z, other % NC), t)
    for d in range(1, NT):
        greet(req, (t + d) % NT)

    def greet_ring(d, carry):
        for e in range(NT):
            greet(index_of(x, (z + d) % NZ, c), (t + e) % NT)
        return carry

    lax.fori_loop(1, NZ, greet_ring, 0)

    kv_lanes = pl.ds(pl.multiple_of((t // 2) * HEAD, HEAD), HEAD)
    slot_start = pl.multiple_of(half * SLOTS, SLOTS)
    loads = [
        pltpu.make_async_copy(queries, qbuf, load_sem.at[0]),
        pltpu.make_async_copy(
            cache_kv.at[:, :, :, kv_lanes], kvbuf.at[:, :, pl.ds(0, CACHE)], load_sem.at[1]
        ),
        pltpu.make_async_copy(
            response_kv.at[:, :, :, kv_lanes], kvbuf.at[:, :, pl.ds(CACHE, RESP)], load_sem.at[2]
        ),
        pltpu.make_async_copy(out_proj, wbuf, load_sem.at[3]),
        pltpu.make_async_copy(residual.at[model, pl.ds(slot_start, SLOTS)], resbuf, load_sem.at[4]),
    ]
    small = [
        (cache_lengths_in, cache_lengths), (sink_count_in, sink_count),
        (window_size_in, window_size), (targets_in, targets), (owner_in, owner),
        (lengths_in, lengths), (gain_in, gain),
    ]
    small = [
        pltpu.make_async_copy(src, dst, load_sem.at[6 + i]) for i, (src, dst) in enumerate(small)
    ]
    own_head = pltpu.make_async_copy(head.at[model], hbuf.at[:, lanes(t)], load_sem.at[5])
    for copy in small + loads:
        copy.start()
    own_head.start()

    req_sub = iota((REQS, ROWS), 0)
    row_lane = iota((REQS, ROWS), 1)
    same_xc = ((req_sub >> 5) == (row_lane >> 7)) & ((req_sub & 1) == ((row_lane >> 4) & 1))
    same_z = ((iota((NZ, REQS), 1) >> 1) & (NZ - 1)) == iota((NZ, REQS), 0)
    zmask = jnp.where(same_z, 1.0, 0.0)

    def piece(k):
        return pl.ds(k * PIECE, PIECE)

    def pair_copy(k):
        return send(
            head.at[model, piece(k)], hbuf.at[piece(k), lanes(t)], hp_s.at[k], hp_r.at[k], req, pair
        )

    def across_copy(k):
        return send(
            head.at[1 - model, piece(k)], hbuf.at[piece(k), lanes(t)], hq_s.at[k], hq_r.at[k],
            req, across,
        )

    def across_recv(k):
        return send(
            head.at[1 - model, piece(k)], hbuf.at[piece(k), lanes(across)], hq_s.at[k], hq_r.at[k],
            req, across,
        )

    def forward_copy(k):
        part = hbuf.at[piece(k), lanes(across)]
        return send(part, part, hf_s.at[k], hf_r.at[k], req, pair)

    def pair_recv(k):
        part = hbuf.at[piece(k), lanes(pair)]
        return send(part, part, hp_s.at[k], hp_r.at[k], req, pair)

    def forward_recv(k):
        part = hbuf.at[piece(k), lanes(NT - 1 - pair)]
        return send(part, part, hf_s.at[k], hf_r.at[k], req, pair)

    for copy in small + loads[:3]:
        copy.wait()
    length = cache_lengths[...]
    stack = (GROUP * RESP, KEYS)
    query_pos = length + (iota(stack, 0) & (RESP - 1))
    key = iota(stack, 1)
    key_pos = jnp.where(key < CACHE, key, length + key - CACHE)
    key_live = (key >= CACHE) | (key < length)
    inside = (key_pos < sink_count[...]) | (query_pos - key_pos < window_size[...])
    allowed = key_live & (key_pos <= query_pos) & inside
    for m in range(2):
        stacked = jnp.concatenate(
            [qbuf[m, 0, :, HEAD * g : HEAD * g + HEAD] for g in range(GROUP)], axis=0
        )
        scores = nt_dot(stacked, kvbuf[m, 0]) * HEAD ** (-0.5)
        masked = jnp.where(allowed, scores, -jnp.inf)
        weights = jnp.exp(masked - jnp.max(masked, axis=-1, keepdims=True))
        weights = (weights / jnp.sum(weights, axis=-1, keepdims=True)).astype(jnp.bfloat16)
        attended = jnp.dot(weights, kvbuf[m, 1], preferred_element_type=jnp.float32)
        attended = attended.astype(jnp.bfloat16)
        for g in range(GROUP):
            attbuf[m, :, HEAD * g : HEAD * g + HEAD] = attended[RESP * g : RESP * g + RESP]
    loads[3].wait()
    for m in range(2):
        partial[m] = jnp.dot(attbuf[m], wbuf[m], preferred_element_type=jnp.float32)

    pl.semaphore_wait(barrier, (NX * NC - 1) + (NT * NZ - 1))

    def rs_copy(d):
        pt = (t + d) % NT
        start = pl.multiple_of((pt % 2) * SLOTS, SLOTS)
        return send(
            partial.at[pt // 2, pl.ds(start, SLOTS)], rs_in.at[d], rs_s.at[d], rs_r.at[d], req, pt
        )

    for d in range(1, NT):
        rs_copy(d).start()
    for k in range(PIECES):
        if k < 2:
            pair_copy(k).start()
        across_copy(k).start()

    lane128 = iota((REQS, 128), 1)
    sub128 = iota((REQS, 128), 0)
    same_xc_lane = ((sub128 >> 5) == (lane128 >> 5)) & ((sub128 & 1) == ((lane128 >> 4) & 1))
    wide = jnp.concatenate(
        [zmask * targets[s : s + 1, :].astype(jnp.float32) for s in range(8)], axis=0
    )
    wide = jnp.dot(
        wide, jnp.where(same_xc_lane, 1.0, 0.0), precision=EXACT,
        preferred_element_type=jnp.float32,
    )
    slot_lane = iota((NZ, 128), 1) & (SLOTS - 1)
    placed = jnp.zeros((NZ, 128), jnp.float32)
    for s in range(8):
        placed = jnp.where(slot_lane == s + 8 * half, wide[NZ * s : NZ * s + NZ], placed)
    tgt_in[0] = placed.astype(jnp.int32)

    def tgt_copy(d):
        return send(tgt_in.at[0], tgt_in.at[d], tg_s.at[d], tg_r.at[d], req, (t + d) % NT)

    for d in range(1, NT):
        tgt_copy(d).start()
    own_all[...] = jnp.dot(
        zmask * owner[...].astype(jnp.float32), jnp.where(same_xc, 1.0, 0.0), precision=EXACT,
        preferred_element_type=jnp.float32,
    ).astype(jnp.int32)

    def forward_head(k):
        across_recv(k).wait_recv()
        forward_copy(k).start()
        if k < 2:
            pair_copy(k + 2).start()

    loads[4].wait()
    hidden = resbuf[...].astype(jnp.float32)
    total = partial[model, pl.ds(slot_start, SLOTS), :]
    for d in range(1, NT):
        rs_copy(d).wait_recv()
        total = total + rs_in[d]
    hidden = hidden + total
    scale_inv = lax.rsqrt(jnp.mean(hidden * hidden, axis=-1, keepdims=True) + 1e-06)
    rows[x, OWN, c] = (hidden * scale_inv * gain[pl.ds(model, 1), :]).astype(jnp.bfloat16)

    steps = range(1, 5)
    streams = [(side, j) for side in range(2) for j in range(2)]

    def slot_of(k, side, j):
        return 4 * (k - 1) + 2 * side + j

    def exists(k, side, j):
        return slot_of(k, side, j) != OWN

    def away(side, hops):
        return index_of(x, (z + hops) % NZ if side == 0 else (z + NZ - hops) % NZ, c)

    targets_of = [[away(side, 1), away(side, 2)] for side in range(2)]

    def z_copy(k, side, j):
        src = OWN if k == 1 else slot_of(k - 1, side, j)
        dst = slot_of(k, side, j)
        to = targets_of[side][j if k == 1 else 1]
        return send(rows.at[x, src, c], rows.at[x, dst, c], z_s.at[dst], z_r.at[dst], to, t)

    beside = [index_of((x + d) % NX, z, c) for d in range(NX)]
    twin = index_of(x, z, 1 - c)

    groups = [(OWN, 1)] + [(4 * (k - 1) + 2 * side, 2) for k in steps for side in range(2)]
    groups[8] = (OWN - 1, 1)

    def x_part(g, block, part_lanes):
        start, size = groups[g]
        return rows.at[(x + block) % NX, pl.ds(start, size), c, :, part_lanes]

    def x_copy(g, way, second, receiving=False):
        back = NX - 1 if way == 0 else 1
        block = (back if second else 0) + (back if receiving else 0)
        part = x_part(g, block, FEATURE_HALVES[way] if second else ALL)
        n = 4 * g + 2 * second + way
        return send(part, part, x_s.at[n], x_r.at[n], beside[1 if way == 0 else NX - 1], t)

    def twin_copy(g, core):
        start, size = groups[g]
        part = rows.at[:, pl.ds(start, size), core]
        return send(part, part, c_s.at[g], c_r.at[g], twin, t)

    def x_send(g):
        for way in range(2):
            x_copy(g, way, 0).start()

    def x_pass(g):
        for way in range(2):
            x_copy(g, way, 0, True).wait_recv()
            x_copy(g, way, 1).start()

    def x_done(g):
        for way in range(2):
            x_copy(g, way, 1, True).wait_recv()
        twin_copy(g, c).start()

    def other_core(*gs):
        for g in gs:
            twin_copy(g, 1 - c).wait_recv()

    def arrive(k):
        for side in range(2):
            for j in range(2):
                if not exists(k, side, j):
                    continue
                z_copy(k, side, j).wait_recv()
                if k < 4 and exists(k + 1, side, j):
                    z_copy(k + 1, side, j).start()
            x_send(2 * k - 1 + side)

    for j in range(2):
        for side in range(2):
            z_copy(1, side, j).start()
    x_send(0)
    forward_head(0)

    tgt_own = jnp.zeros((NZ, 128), jnp.int32)
    for d in range(NT):
        if d:
            tgt_copy(d).wait_recv()
        wanted_half = ((t + NT - d) % NT) // 2 == half
        tgt_own = tgt_own + jnp.where(wanted_half, tgt_in[d], 0)
    small_lane = ((iota((128, ROWS), 1) >> 7) << 5) + (iota((128, ROWS), 1) & 31)
    repeat = jnp.where(small_lane == iota((128, ROWS), 0), 1.0, 0.0)
    tgt_wide = jnp.dot(
        tgt_own.astype(jnp.float32), repeat, precision=EXACT, preferred_element_type=jnp.float32
    )
    tgt_all[...] = tgt_wide.astype(jnp.int32) - req * VOCAB_BLOCK
    outbuf[...] = jnp.zeros_like(outbuf)
    peak_buf[...] = jnp.full_like(peak_buf, -jnp.inf)
    norm_buf[...] = jnp.zeros_like(norm_buf)
    pick_buf[...] = jnp.zeros_like(pick_buf)

    def prepare(k):
        near, far = 2 * k + 1, 2 * k + 2
        places = [(z + NZ - near) % NZ, (z + NZ - far) % NZ, (z + near) % NZ, (z + far % 8) % NZ]
        place = (iota((1, ROWS), 1) >> 5) & 3

        def pick(table):
            found = table[pl.ds(places[3], 1), :]
            for i in range(3):
                found = jnp.where(place == i, table[pl.ds(places[i], 1), :], found)
            return found

        wanted_buf[k] = pick(tgt_all)
        sub = iota((REQS, ROWS), 0)
        dest = ((sub >> 5) * NZ + (sub & (NZ - 1))) * NC + ((sub >> 4) & 1)
        select_buf[k] = jnp.where(dest == pick(own_all), 1.0, 0.0).astype(jnp.bfloat16)

    def head_ready(k):
        pair_recv(k).wait_recv()
        forward_recv(k).wait_recv()

    def units(k0, k1, p0, p1):
        def unit(i, carry):
            k = k0 + i // (p1 - p0)
            p = p0 + i % (p1 - p0)
            base = pl.multiple_of(p * BLOCK, BLOCK)
            chunk = rows[:, pl.ds(4 * k, 4)].reshape(ROWS, D)
            logits = nt_dot(hbuf[pl.ds(base, BLOCK), :], chunk)
            peak = jnp.max(logits, axis=0, keepdims=True)
            hit = iota((BLOCK, ROWS), 0) == wanted_buf[k] - base
            pick_buf[k] += jnp.sum(jnp.where(hit, logits, 0.0), axis=0, keepdims=True)
            old = peak_buf[k]
            new = jnp.maximum(old, peak)
            norm = jnp.sum(jnp.exp(logits - new), axis=0, keepdims=True)
            norm_buf[k] = norm_buf[k] * jnp.exp(old - new) + norm
            peak_buf[k] = new
            return carry

        lax.fori_loop(0, (k1 - k0) * (p1 - p0), unit, 0)

    arrive(1)
    x_pass(0)
    forward_head(1)
    prepare(0)
    prepare(1)

    arrive(2)
    x_pass(1)
    x_pass(2)
    forward_head(2)
    x_done(0)
    prepare(2)
    prepare(3)

    arrive(3)
    x_pass(3)
    x_pass(4)
    forward_head(3)
    x_done(1)
    x_done(2)

    arrive(4)
    x_pass(5)
    x_pass(6)
    x_done(3)
    x_done(4)
    own_head.wait()
    head_ready(0)
    head_ready(1)
    other_core(1, 2)
    units(0, 1, 0, 1)
    x_pass(7)
    x_pass(8)
    x_done(5)
    x_done(6)
    other_core(3, 4)
    units(1, 2, 0, 1)
    other_core(5, 6)
    units(2, 3, 0, 1)
    x_done(7)
    x_done(8)
    head_ready(2)
    head_ready(3)
    units(0, 3, 1, 2)
    other_core(7, 8, 0)
    units(3, 4, 0, 2)

    def finish(k, carry):
        sub = iota((2 * SLOTS, ROWS), 0)
        slot = iota((2 * SLOTS, ROWS), 1) & (SLOTS - 1)
        lse = peak_buf[k] + jnp.log(norm_buf[k])
        values = jnp.where(sub == slot, lse, jnp.where(sub == slot + SLOTS, pick_buf[k], 0.0))
        terms = []
        for _ in range(3):
            terms.append(values.astype(jnp.bfloat16))
            values = values - terms[-1].astype(jnp.float32)
        terms.append(jnp.zeros_like(terms[0]))
        outbuf[...] += nt_dot(select_buf[k], jnp.concatenate(terms, axis=0))
        return carry

    lax.fori_loop(0, CHUNKS, finish, 0)
    found = outbuf[...]
    outbuf[...] = (found + pltpu.roll(found, 96, 1)) + pltpu.roll(found, 64, 1)

    def e1_copy(d):
        other = (group + d) % (NX * NC)
        return send(
            outbuf.at[pl.ds(pl.multiple_of(other * NZ, NZ), NZ)], in1.at[d], e1_s.at[d], e1_r.at[d],
            index_of(other // NC, z, other % NC), t,
        )

    for d in range(1, NX * NC):
        e1_copy(d).start()
    in1[0] = outbuf[pl.ds(pl.multiple_of(group * NZ, NZ), NZ), :]
    for d in range(1, NX * NC):
        e1_copy(d).wait_recv()

    def combine(values):
        peak = jnp.max(values, axis=0, keepdims=True)
        lse = peak + jnp.log(jnp.sum(jnp.exp(values - peak), axis=0, keepdims=True))
        pick = jnp.sum(values, axis=0, keepdims=True)
        return jnp.where(iota(lse.shape, 2) < SLOTS, lse, pick)[0]

    merged = combine(in1[...])
    for k in range(NZ):
        ex2[k] = merged[k : k + 1]

    def e2_copy(d, e):
        pz = (z + d) % NZ
        n = NT * d + e
        return send(
            ex2.at[pz], in2.at[t, d], e2_s.at[n], e2_r.at[n], index_of(x, pz, c), (t + e) % NT
        )

    def e2_recv(d, e):
        n = NT * d + e
        dst = in2.at[(t + NT - e) % NT, d]
        return send(ex2.at[0], dst, e2_s.at[n], e2_r.at[n], index_of(x, (z + d) % NZ, c), (t + e) % NT)

    def ring_loop(body):
        def step(d, carry):
            for e in range(NT):
                body(d, e)
            return carry

        for e in range(1, NT):
            body(0, e)
        lax.fori_loop(1, NZ, step, 0)

    ring_loop(lambda d, e: e2_copy(d, e).start())
    in2[t, 0] = ex2[z]
    count = jnp.sum(jnp.where(owner[...] == req, lengths[...], 0), axis=1, keepdims=True)
    ring_loop(lambda d, e: e2_recv(d, e).wait_recv())
    for column in range(NT):
        final = combine(in2[column])
        in3[column] = pltpu.roll(final, 128 - SLOTS, 1) - final
    lane = iota((1, 128), 1)
    live0 = (lane < SLOTS) & (lane < count)
    live1 = (lane < SLOTS) & (lane + SLOTS < count)
    low, high = in3[0], in3[1]
    policy_total = jnp.sum(
        jnp.where(live0, low, 0.0) + jnp.where(live1, high, 0.0), axis=1, keepdims=True
    )
    ratio_total = jnp.sum(
        jnp.where(live0, low - in3[2], 0.0) + jnp.where(live1, high - in3[3], 0.0),
        axis=1, keepdims=True,
    )
    counts = count.astype(jnp.float32)
    scores = jnp.where(lane == 0, policy_total / counts, ratio_total / counts)
    scores_out[...] = scores[:, 0:2]
    mine = in3[t // 2]
    mine = jnp.where(half == 1, pltpu.roll(mine, 120, 1), mine)
    mine = jnp.where(lane + 8 * t < count, mine, 0.0)
    policy_out[...] = mine[:, 0:8]

    for d in range(1, NT):
        rs_copy(d).wait_send()
        tgt_copy(d).wait_send()
    for k in steps:
        for side, j in streams:
            if exists(k, side, j):
                z_copy(k, side, j).wait_send()
    for g in range(9):
        for way in range(2):
            x_copy(g, way, 0).wait_send()
            x_copy(g, way, 1).wait_send()
        twin_copy(g, c).wait_send()

    def head_sent(k, carry):
        pair_copy(k).wait_send()
        across_copy(k).wait_send()
        forward_copy(k).wait_send()
        return carry

    lax.fori_loop(0, PIECES, head_sent, 0)

    for d in range(1, NX * NC):
        e1_copy(d).wait_send()
    ring_loop(lambda d, e: e2_copy(d, e).wait_send())


def per_device(
    queries,
    response_kv,
    cache_kv,
    residual,
    out_proj,
    norm_gain,
    lm_head,
    targets,
    resp_lengths,
    cache_lengths,
    owner_slot,
    sink_count,
    window_size,
):
    dma = pltpu.SemaphoreType.DMA
    vmem = pl.BlockSpec(memory_space=pltpu.VMEM)
    hbm = pl.BlockSpec(memory_space=pltpu.HBM)
    semaphores = [13] + [NT] * 4 + [PIECES] * 6 + [16] * 2 + [36] * 2
    semaphores += [9] * 2 + [8] * 2 + [NZ * NT] * 2
    bf16, f32, i32 = jnp.bfloat16, jnp.float32, jnp.int32
    return pl.pallas_call(
        fused,
        out_shape=(jax.ShapeDtypeStruct((1, 8), f32), jax.ShapeDtypeStruct((1, 2), f32)),
        in_specs=[hbm] * 13,
        out_specs=(vmem, vmem),
        scratch_shapes=[
            pltpu.VMEM((2, D), f32),
            pltpu.VMEM((RESP // NT, REQS), i32),
            pltpu.VMEM((1, REQS), i32),
            pltpu.VMEM((1, REQS), i32),
            pltpu.VMEM((1, 1), i32),
            pltpu.VMEM((1, 1), i32),
            pltpu.VMEM((1, 1), i32),
            pltpu.VMEM((2, 1, RESP, FEAT), bf16),
            pltpu.VMEM((2, 2, KEYS, HEAD), bf16),
            pltpu.VMEM((2, FEAT, D), bf16),
            pltpu.VMEM((SLOTS, D), bf16),
            pltpu.VMEM((2, RESP, FEAT), bf16),
            pltpu.VMEM((2, RESP, D), f32),
            pltpu.VMEM((VOCAB_BLOCK, D), bf16),
            pltpu.VMEM((NX, NZ, NC, SLOTS, D), bf16),
            pltpu.VMEM((NT, SLOTS, D), f32),
            pltpu.VMEM((NT, NZ, 128), i32),
            pltpu.VMEM((NZ, ROWS), i32),
            pltpu.VMEM((NZ, ROWS), i32),
            pltpu.VMEM((CHUNKS, 1, ROWS), i32),
            pltpu.VMEM((CHUNKS, REQS, ROWS), bf16),
            pltpu.VMEM((CHUNKS, 1, ROWS), f32),
            pltpu.VMEM((CHUNKS, 1, ROWS), f32),
            pltpu.VMEM((CHUNKS, 1, ROWS), f32),
            pltpu.VMEM((REQS, 128), f32),
            pltpu.VMEM((NX * NC, NZ, 128), f32),
            pltpu.VMEM((NZ, 1, 128), f32),
            pltpu.VMEM((NT, NZ, 1, 128), f32),
            pltpu.VMEM((NT, 1, 128), f32),
        ]
        + [dma((n,)) for n in semaphores],
        compiler_params=pltpu.CompilerParams(
            collective_id=0, has_side_effects=True, vmem_limit_bytes=63 << 20
        ),
    )(
        queries,
        response_kv.reshape(2, 2, RESP, KV_HEADS * HEAD),
        cache_kv.reshape(2, 2, CACHE, KV_HEADS * HEAD),
        residual.reshape(2, RESP, D),
        out_proj,
        norm_gain,
        lm_head,
        targets.T,
        resp_lengths.reshape(1, REQS),
        owner_slot.reshape(1, REQS),
        cache_lengths.reshape(1, 1),
        sink_count.reshape(1, 1),
        window_size.reshape(1, 1),
    )


def solution(mesh):
    in_specs = (
        P(None, "req", None, "tp"),
        P(None, "req", None, None, None),
        P(None, "req", None, None, None),
        P(None, "req", None, None),
        P(None, "tp", None),
        P(),
        P(None, "req", "tp"),
        P(None, "tp"),
        P(),
        P("req"),
        P(),
        P(),
        P(),
    )
    out_specs = (P("req", "tp"), P("req", None))
    return jax.shard_map(
        per_device, mesh=mesh, in_specs=in_specs, out_specs=out_specs, check_vma=False
    )
```

```python
import jax
import jax.numpy as jnp
from jax import lax
from jax.experimental import pallas as pl
from jax.experimental.pallas import tpu as pltpu
from jax.sharding import PartitionSpec as P

HEADS = 12
HEAD = 128
KV_HEADS = 2
RESP = 32
CACHE = 384
KEYS = CACHE + RESP
D = 1536

NX, NZ, NC, NT = 4, 16, 2, 4
REQS = NX * NZ * NC
SLOTS = 16
FEAT = D // NT
GROUP = HEADS // NT
VOCAB_BLOCK = 1024
PIECES = 4
PIECE = VOCAB_BLOCK // PIECES
CHUNKS = 4
ROWS = 4 * NX * NC * SLOTS
BLOCK = 512
FEATURE_HALVES = (pl.ds(0, D // 2), pl.ds(D // 2, D // 2))
ALL = pl.ds(0, D)
OWN = 4 * 4 - 1
MESH = pl.DeviceIdType.MESH
EXACT = lax.Precision.HIGHEST


def iota(shape, dim):
    return lax.broadcasted_iota(jnp.int32, shape, dim)


def nt_dot(a, b, precision=None):
    return lax.dot_general(
        a, b, (((1,), (1,)), ((), ())), precision=precision, preferred_element_type=jnp.float32
    )


def fused(
    queries, response_kv, cache_kv, residual, out_proj, gain_in, head, targets_in, lengths_in,
    owner_in, cache_lengths_in, sink_count_in, window_size_in,
    policy_out, scores_out,
    gain, targets, lengths, owner, cache_lengths, sink_count, window_size,
    qbuf, kvbuf, wbuf, resbuf, attbuf, partial,
    hbuf, rows, rs_in, tgt_in, tgt_all, own_all, wanted_buf, select_buf,
    peak_buf, norm_buf, pick_buf, outbuf, in1, ex2, in2, in3,
    load_sem, rs_s, rs_r, tg_s, tg_r, hp_s, hp_r, hq_s, hq_r, hf_s, hf_r,
    z_s, z_r, x_s, x_r, c_s, c_r, e1_s, e1_r, e2_s, e2_r,
):
    req = lax.axis_index("req")
    t = lax.axis_index("tp")
    x = req // (NZ * NC)
    z = (req // NC) % NZ
    c = req % NC
    model = t // 2
    half = t % 2
    pair = t + 1 - 2 * (t % 2)
    across = NT - 1 - t
    group = x * NC + c

    def index_of(px, pz, pc):
        return (px * NZ + pz) * NC + pc

    def send(src, dst, ssem, rsem, preq, pt):
        return pltpu.make_async_remote_copy(
            src_ref=src, dst_ref=dst, send_sem=ssem, recv_sem=rsem,
            device_id={"req": preq, "tp": pt}, device_id_type=MESH,
        )

    def lanes(source):
        return pl.ds(pl.multiple_of(source * FEAT, FEAT), FEAT)

    barrier = pltpu.get_barrier_semaphore()

    def greet(preq, pt):
        pl.semaphore_signal(
            barrier, inc=1, device_id={"req": preq, "tp": pt}, device_id_type=MESH
        )

    for d in range(1, NX * NC):
        other = (group + d) % (NX * NC)
        greet(index_of(other // NC, z, other % NC), t)
    for d in range(1, NT):
        greet(req, (t + d) % NT)

    def greet_ring(d, carry):
        for e in range(NT):
            greet(index_of(x, (z + d) % NZ, c), (t + e) % NT)
        return carry

    lax.fori_loop(1, NZ, greet_ring, 0)

    kv_lanes = pl.ds(pl.multiple_of((t // 2) * HEAD, HEAD), HEAD)
    slot_start = pl.multiple_of(half * SLOTS, SLOTS)
    loads = [
        pltpu.make_async_copy(queries, qbuf, load_sem.at[0]),
        pltpu.make_async_copy(
            cache_kv.at[:, :, :, kv_lanes], kvbuf.at[:, :, pl.ds(0, CACHE)], load_sem.at[1]
        ),
        pltpu.make_async_copy(
            response_kv.at[:, :, :, kv_lanes], kvbuf.at[:, :, pl.ds(CACHE, RESP)], load_sem.at[2]
        ),
        pltpu.make_async_copy(out_proj, wbuf, load_sem.at[3]),
        pltpu.make_async_copy(residual.at[model, pl.ds(slot_start, SLOTS)], resbuf, load_sem.at[4]),
    ]
    small = [
        (cache_lengths_in, cache_lengths), (sink_count_in, sink_count),
        (window_size_in, window_size), (targets_in, targets), (owner_in, owner),
        (lengths_in, lengths), (gain_in, gain),
    ]
    small = [
        pltpu.make_async_copy(src, dst, load_sem.at[6 + i]) for i, (src, dst) in enumerate(small)
    ]
    own_head = pltpu.make_async_copy(head.at[model], hbuf.at[:, lanes(t)], load_sem.at[5])
    for copy in small + loads:
        copy.start()
    own_head.start()

    req_sub = iota((REQS, ROWS), 0)
    row_lane = iota((REQS, ROWS), 1)
    same_xc = ((req_sub >> 5) == (row_lane >> 7)) & ((req_sub & 1) == ((row_lane >> 4) & 1))
    same_z = ((iota((NZ, REQS), 1) >> 1) & (NZ - 1)) == iota((NZ, REQS), 0)
    zmask = jnp.where(same_z, 1.0, 0.0)

    pl.semaphore_wait(barrier, (NX * NC - 1) + (NT * NZ - 1))

    def piece(k):
        return pl.ds(k * PIECE, PIECE)

    def pair_copy(k):
        return send(
            head.at[model, piece(k)], hbuf.at[piece(k), lanes(t)], hp_s.at[k], hp_r.at[k], req, pair
        )

    def across_copy(k):
        return send(
            head.at[1 - model, piece(k)], hbuf.at[piece(k), lanes(t)], hq_s.at[k], hq_r.at[k],
            req, across,
        )

    def across_recv(k):
        return send(
            head.at[1 - model, piece(k)], hbuf.at[piece(k), lanes(across)], hq_s.at[k], hq_r.at[k],
            req, across,
        )

    def forward_copy(k):
        part = hbuf.at[piece(k), lanes(across)]
        return send(part, part, hf_s.at[k], hf_r.at[k], req, pair)

    def pair_recv(k):
        part = hbuf.at[piece(k), lanes(pair)]
        return send(part, part, hp_s.at[k], hp_r.at[k], req, pair)

    def forward_recv(k):
        part = hbuf.at[piece(k), lanes(NT - 1 - pair)]
        return send(part, part, hf_s.at[k], hf_r.at[k], req, pair)

    across_copy(0).start()
    pair_copy(0).start()
    across_copy(1).start()

    for copy in small + loads[:3]:
        copy.wait()
    length = cache_lengths[...]
    stack = (GROUP * RESP, KEYS)
    query_pos = length + (iota(stack, 0) & (RESP - 1))
    key = iota(stack, 1)
    key_pos = jnp.where(key < CACHE, key, length + key - CACHE)
    key_live = (key >= CACHE) | (key < length)
    inside = (key_pos < sink_count[...]) | (query_pos - key_pos < window_size[...])
    allowed = key_live & (key_pos <= query_pos) & inside
    for m in range(2):
        stacked = jnp.concatenate(
            [qbuf[m, 0, :, HEAD * g : HEAD * g + HEAD] for g in range(GROUP)], axis=0
        )
        scores = nt_dot(stacked, kvbuf[m, 0]) * HEAD ** (-0.5)
        masked = jnp.where(allowed, scores, -jnp.inf)
        weights = jnp.exp(masked - jnp.max(masked, axis=-1, keepdims=True))
        weights = (weights / jnp.sum(weights, axis=-1, keepdims=True)).astype(jnp.bfloat16)
        attended = jnp.dot(weights, kvbuf[m, 1], preferred_element_type=jnp.float32)
        attended = attended.astype(jnp.bfloat16)
        for g in range(GROUP):
            attbuf[m, :, HEAD * g : HEAD * g + HEAD] = attended[RESP * g : RESP * g + RESP]
    loads[3].wait()
    for m in range(2):
        partial[m] = jnp.dot(attbuf[m], wbuf[m], preferred_element_type=jnp.float32)

    def rs_copy(d):
        pt = (t + d) % NT
        start = pl.multiple_of((pt % 2) * SLOTS, SLOTS)
        return send(
            partial.at[pt // 2, pl.ds(start, SLOTS)], rs_in.at[d], rs_s.at[d], rs_r.at[d], req, pt
        )

    for d in range(1, NT):
        rs_copy(d).start()

    lane128 = iota((REQS, 128), 1)
    sub128 = iota((REQS, 128), 0)
    same_xc_lane = ((sub128 >> 5) == (lane128 >> 5)) & ((sub128 & 1) == ((lane128 >> 4) & 1))
    wide = jnp.concatenate(
        [zmask * targets[s : s + 1, :].astype(jnp.float32) for s in range(8)], axis=0
    )
    wide = jnp.dot(
        wide, jnp.where(same_xc_lane, 1.0, 0.0), precision=EXACT,
        preferred_element_type=jnp.float32,
    )
    slot_lane = iota((NZ, 128), 1) & (SLOTS - 1)
    placed = jnp.zeros((NZ, 128), jnp.float32)
    for s in range(8):
        placed = jnp.where(slot_lane == s + 8 * half, wide[NZ * s : NZ * s + NZ], placed)
    tgt_in[0] = placed.astype(jnp.int32)

    def tgt_copy(d):
        return send(tgt_in.at[0], tgt_in.at[d], tg_s.at[d], tg_r.at[d], req, (t + d) % NT)

    for d in range(1, NT):
        tgt_copy(d).start()
    own_all[...] = jnp.dot(
        zmask * owner[...].astype(jnp.float32), jnp.where(same_xc, 1.0, 0.0), precision=EXACT,
        preferred_element_type=jnp.float32,
    ).astype(jnp.int32)

    def forward_head(k):
        across_recv(k).wait_recv()
        forward_copy(k).start()
        if k in (1, 2):
            pair_copy(k + 1).start()

    pair_copy(1).start()
    across_copy(2).start()
    forward_head(0)
    across_copy(3).start()

    loads[4].wait()
    hidden = resbuf[...].astype(jnp.float32)
    total = partial[model, pl.ds(slot_start, SLOTS), :]
    for d in range(1, NT):
        rs_copy(d).wait_recv()
        total = total + rs_in[d]
    hidden = hidden + total
    scale_inv = lax.rsqrt(jnp.mean(hidden * hidden, axis=-1, keepdims=True) + 1e-06)
    rows[x, OWN, c] = (hidden * scale_inv * gain[pl.ds(model, 1), :]).astype(jnp.bfloat16)

    steps = range(1, 5)
    streams = [(side, j) for side in range(2) for j in range(2)]

    def slot_of(k, side, j):
        return 4 * (k - 1) + 2 * side + j

    def exists(k, side, j):
        return slot_of(k, side, j) != OWN

    def away(side, hops):
        return index_of(x, (z + hops) % NZ if side == 0 else (z + NZ - hops) % NZ, c)

    targets_of = [[away(side, 1), away(side, 2)] for side in range(2)]

    def z_copy(k, side, j):
        src = OWN if k == 1 else slot_of(k - 1, side, j)
        dst = slot_of(k, side, j)
        to = targets_of[side][j if k == 1 else 1]
        return send(rows.at[x, src, c], rows.at[x, dst, c], z_s.at[dst], z_r.at[dst], to, t)

    beside = [index_of((x + d) % NX, z, c) for d in range(NX)]
    twin = index_of(x, z, 1 - c)

    groups = [(OWN, 1)] + [(4 * (k - 1) + 2 * side, 2) for k in steps for side in range(2)]
    groups[8] = (OWN - 1, 1)

    def x_part(g, block, part_lanes):
        start, size = groups[g]
        return rows.at[(x + block) % NX, pl.ds(start, size), c, :, part_lanes]

    def x_copy(g, way, second, receiving=False):
        back = NX - 1 if way == 0 else 1
        block = (back if second else 0) + (back if receiving else 0)
        part = x_part(g, block, FEATURE_HALVES[way] if second else ALL)
        n = 4 * g + 2 * second + way
        return send(part, part, x_s.at[n], x_r.at[n], beside[1 if way == 0 else NX - 1], t)

    def twin_copy(g, core):
        start, size = groups[g]
        part = rows.at[:, pl.ds(start, size), core]
        return send(part, part, c_s.at[g], c_r.at[g], twin, t)

    def x_send(g):
        for way in range(2):
            x_copy(g, way, 0).start()

    def x_pass(g):
        for way in range(2):
            x_copy(g, way, 0, True).wait_recv()
            x_copy(g, way, 1).start()

    def x_done(g):
        for way in range(2):
            x_copy(g, way, 1, True).wait_recv()
        twin_copy(g, c).start()

    def other_core(*gs):
        for g in gs:
            twin_copy(g, 1 - c).wait_recv()

    def arrive(k):
        for side in range(2):
            for j in range(2):
                if not exists(k, side, j):
                    continue
                z_copy(k, side, j).wait_recv()
                if k < 4 and exists(k + 1, side, j):
                    z_copy(k + 1, side, j).start()
            x_send(2 * k - 1 + side)

    for j in range(2):
        for side in range(2):
            z_copy(1, side, j).start()
    x_send(0)
    forward_head(1)

    tgt_own = jnp.zeros((NZ, 128), jnp.int32)
    for d in range(NT):
        if d:
            tgt_copy(d).wait_recv()
        wanted_half = ((t + NT - d) % NT) // 2 == half
        tgt_own = tgt_own + jnp.where(wanted_half, tgt_in[d], 0)
    small_lane = ((iota((128, ROWS), 1) >> 7) << 5) + (iota((128, ROWS), 1) & 31)
    repeat = jnp.where(small_lane == iota((128, ROWS), 0), 1.0, 0.0)
    tgt_wide = jnp.dot(
        tgt_own.astype(jnp.float32), repeat, precision=EXACT, preferred_element_type=jnp.float32
    )
    tgt_all[...] = tgt_wide.astype(jnp.int32) - req * VOCAB_BLOCK
    outbuf[...] = jnp.zeros_like(outbuf)
    peak_buf[...] = jnp.full_like(peak_buf, -jnp.inf)
    norm_buf[...] = jnp.zeros_like(norm_buf)
    pick_buf[...] = jnp.zeros_like(pick_buf)

    def prepare(k):
        near, far = 2 * k + 1, 2 * k + 2
        places = [(z + NZ - near) % NZ, (z + NZ - far) % NZ, (z + near) % NZ, (z + far % 8) % NZ]
        place = (iota((1, ROWS), 1) >> 5) & 3

        def pick(table):
            found = table[pl.ds(places[3], 1), :]
            for i in range(3):
                found = jnp.where(place == i, table[pl.ds(places[i], 1), :], found)
            return found

        wanted_buf[k] = pick(tgt_all)
        sub = iota((REQS, ROWS), 0)
        dest = ((sub >> 5) * NZ + (sub & (NZ - 1))) * NC + ((sub >> 4) & 1)
        select_buf[k] = jnp.where(dest == pick(own_all), 1.0, 0.0).astype(jnp.bfloat16)

    def head_ready(k):
        pair_recv(k).wait_recv()
        forward_recv(k).wait_recv()

    def units(k0, k1, p0, p1):
        def unit(i, carry):
            k = k0 + i // (p1 - p0)
            p = p0 + i % (p1 - p0)
            base = pl.multiple_of(p * BLOCK, BLOCK)
            chunk = rows[:, pl.ds(4 * k, 4)].reshape(ROWS, D)
            logits = nt_dot(hbuf[pl.ds(base, BLOCK), :], chunk)
            peak = jnp.max(logits, axis=0, keepdims=True)
            hit = iota((BLOCK, ROWS), 0) == wanted_buf[k] - base
            pick_buf[k] += jnp.sum(jnp.where(hit, logits, 0.0), axis=0, keepdims=True)
            old = peak_buf[k]
            new = jnp.maximum(old, peak)
            norm = jnp.sum(jnp.exp(logits - new), axis=0, keepdims=True)
            norm_buf[k] = norm_buf[k] * jnp.exp(old - new) + norm
            peak_buf[k] = new
            return carry

        lax.fori_loop(0, (k1 - k0) * (p1 - p0), unit, 0)

    arrive(1)
    x_pass(0)
    forward_head(2)
    prepare(0)
    prepare(1)

    arrive(2)
    x_pass(1)
    x_pass(2)
    x_done(0)
    forward_head(3)
    prepare(2)
    prepare(3)

    arrive(3)
    x_pass(3)
    x_pass(4)
    x_done(1)
    x_done(2)
    own_head.wait()
    head_ready(0)
    head_ready(1)

    arrive(4)
    x_pass(5)
    x_pass(6)
    x_done(3)
    x_done(4)
    other_core(1, 2)
    units(0, 1, 0, 1)
    x_pass(7)
    x_pass(8)
    x_done(5)
    x_done(6)
    other_core(3, 4)
    units(1, 2, 0, 1)
    x_done(7)
    x_done(8)
    other_core(5, 6)
    units(2, 3, 0, 1)
    head_ready(2)
    head_ready(3)
    units(0, 3, 1, 2)
    other_core(7, 8, 0)
    units(3, 4, 0, 2)

    def finish(k, carry):
        sub = iota((2 * SLOTS, ROWS), 0)
        slot = iota((2 * SLOTS, ROWS), 1) & (SLOTS - 1)
        lse = peak_buf[k] + jnp.log(norm_buf[k])
        values = jnp.where(sub == slot, lse, jnp.where(sub == slot + SLOTS, pick_buf[k], 0.0))
        terms = []
        for _ in range(3):
            terms.append(values.astype(jnp.bfloat16))
            values = values - terms[-1].astype(jnp.float32)
        terms.append(jnp.zeros_like(terms[0]))
        outbuf[...] += nt_dot(select_buf[k], jnp.concatenate(terms, axis=0))
        return carry

    lax.fori_loop(0, CHUNKS, finish, 0)
    found = outbuf[...]
    outbuf[...] = (found + pltpu.roll(found, 96, 1)) + pltpu.roll(found, 64, 1)

    def e1_copy(d):
        other = (group + d) % (NX * NC)
        return send(
            outbuf.at[pl.ds(pl.multiple_of(other * NZ, NZ), NZ)], in1.at[d], e1_s.at[d], e1_r.at[d],
            index_of(other // NC, z, other % NC), t,
        )

    for d in range(1, NX * NC):
        e1_copy(d).start()
    in1[0] = outbuf[pl.ds(pl.multiple_of(group * NZ, NZ), NZ), :]
    for d in range(1, NX * NC):
        e1_copy(d).wait_recv()

    def combine(values):
        peak = jnp.max(values, axis=0, keepdims=True)
        lse = peak + jnp.log(jnp.sum(jnp.exp(values - peak), axis=0, keepdims=True))
        pick = jnp.sum(values, axis=0, keepdims=True)
        return jnp.where(iota(lse.shape, 2) < SLOTS, lse, pick)[0]

    merged = combine(in1[...])
    for k in range(NZ):
        ex2[k] = merged[k : k + 1]

    def e2_copy(d, e):
        pz = (z + d) % NZ
        n = NT * d + e
        return send(
            ex2.at[pz], in2.at[t, d], e2_s.at[n], e2_r.at[n], index_of(x, pz, c), (t + e) % NT
        )

    def e2_recv(d, e):
        n = NT * d + e
        dst = in2.at[(t + NT - e) % NT, d]
        return send(ex2.at[0], dst, e2_s.at[n], e2_r.at[n], index_of(x, (z + d) % NZ, c), (t + e) % NT)

    def ring_loop(body):
        def step(d, carry):
            for e in range(NT):
                body(d, e)
            return carry

        for e in range(1, NT):
            body(0, e)
        lax.fori_loop(1, NZ, step, 0)

    ring_loop(lambda d, e: e2_copy(d, e).start())
    in2[t, 0] = ex2[z]
    count = jnp.sum(jnp.where(owner[...] == req, lengths[...], 0), axis=1, keepdims=True)
    ring_loop(lambda d, e: e2_recv(d, e).wait_recv())
    for column in range(NT):
        final = combine(in2[column])
        in3[column] = pltpu.roll(final, 128 - SLOTS, 1) - final
    lane = iota((1, 128), 1)
    live0 = (lane < SLOTS) & (lane < count)
    live1 = (lane < SLOTS) & (lane + SLOTS < count)
    low, high = in3[0], in3[1]
    policy_total = jnp.sum(
        jnp.where(live0, low, 0.0) + jnp.where(live1, high, 0.0), axis=1, keepdims=True
    )
    ratio_total = jnp.sum(
        jnp.where(live0, low - in3[2], 0.0) + jnp.where(live1, high - in3[3], 0.0),
        axis=1, keepdims=True,
    )
    counts = count.astype(jnp.float32)
    scores = jnp.where(lane == 0, policy_total / counts, ratio_total / counts)
    scores_out[...] = scores[:, 0:2]
    mine = in3[t // 2]
    mine = jnp.where(half == 1, pltpu.roll(mine, 120, 1), mine)
    mine = jnp.where(lane + 8 * t < count, mine, 0.0)
    policy_out[...] = mine[:, 0:8]

    for d in range(1, NT):
        rs_copy(d).wait_send()
        tgt_copy(d).wait_send()
    for k in steps:
        for side, j in streams:
            if exists(k, side, j):
                z_copy(k, side, j).wait_send()
    for g in range(9):
        for way in range(2):
            x_copy(g, way, 0).wait_send()
            x_copy(g, way, 1).wait_send()
        twin_copy(g, c).wait_send()

    def head_sent(k, carry):
        pair_copy(k).wait_send()
        across_copy(k).wait_send()
        forward_copy(k).wait_send()
        return carry

    lax.fori_loop(0, PIECES, head_sent, 0)

    for d in range(1, NX * NC):
        e1_copy(d).wait_send()
    ring_loop(lambda d, e: e2_copy(d, e).wait_send())


def per_device(
    queries,
    response_kv,
    cache_kv,
    residual,
    out_proj,
    norm_gain,
    lm_head,
    targets,
    resp_lengths,
    cache_lengths,
    owner_slot,
    sink_count,
    window_size,
):
    dma = pltpu.SemaphoreType.DMA
    vmem = pl.BlockSpec(memory_space=pltpu.VMEM)
    hbm = pl.BlockSpec(memory_space=pltpu.HBM)
    semaphores = [13] + [NT] * 4 + [PIECES] * 6 + [16] * 2 + [36] * 2
    semaphores += [9] * 2 + [8] * 2 + [NZ * NT] * 2
    bf16, f32, i32 = jnp.bfloat16, jnp.float32, jnp.int32
    return pl.pallas_call(
        fused,
        out_shape=(jax.ShapeDtypeStruct((1, 8), f32), jax.ShapeDtypeStruct((1, 2), f32)),
        in_specs=[hbm] * 13,
        out_specs=(vmem, vmem),
        scratch_shapes=[
            pltpu.VMEM((2, D), f32),
            pltpu.VMEM((RESP // NT, REQS), i32),
            pltpu.VMEM((1, REQS), i32),
            pltpu.VMEM((1, REQS), i32),
            pltpu.VMEM((1, 1), i32),
            pltpu.VMEM((1, 1), i32),
            pltpu.VMEM((1, 1), i32),
            pltpu.VMEM((2, 1, RESP, FEAT), bf16),
            pltpu.VMEM((2, 2, KEYS, HEAD), bf16),
            pltpu.VMEM((2, FEAT, D), bf16),
            pltpu.VMEM((SLOTS, D), bf16),
            pltpu.VMEM((2, RESP, FEAT), bf16),
            pltpu.VMEM((2, RESP, D), f32),
            pltpu.VMEM((VOCAB_BLOCK, D), bf16),
            pltpu.VMEM((NX, NZ, NC, SLOTS, D), bf16),
            pltpu.VMEM((NT, SLOTS, D), f32),
            pltpu.VMEM((NT, NZ, 128), i32),
            pltpu.VMEM((NZ, ROWS), i32),
            pltpu.VMEM((NZ, ROWS), i32),
            pltpu.VMEM((CHUNKS, 1, ROWS), i32),
            pltpu.VMEM((CHUNKS, REQS, ROWS), bf16),
            pltpu.VMEM((CHUNKS, 1, ROWS), f32),
            pltpu.VMEM((CHUNKS, 1, ROWS), f32),
            pltpu.VMEM((CHUNKS, 1, ROWS), f32),
            pltpu.VMEM((REQS, 128), f32),
            pltpu.VMEM((NX * NC, NZ, 128), f32),
            pltpu.VMEM((NZ, 1, 128), f32),
            pltpu.VMEM((NT, NZ, 1, 128), f32),
            pltpu.VMEM((NT, 1, 128), f32),
        ]
        + [dma((n,)) for n in semaphores],
        compiler_params=pltpu.CompilerParams(
            collective_id=0, has_side_effects=True, vmem_limit_bytes=63 << 20
        ),
    )(
        queries,
        response_kv.reshape(2, 2, RESP, KV_HEADS * HEAD),
        cache_kv.reshape(2, 2, CACHE, KV_HEADS * HEAD),
        residual.reshape(2, RESP, D),
        out_proj,
        norm_gain,
        lm_head,
        targets.T,
        resp_lengths.reshape(1, REQS),
        owner_slot.reshape(1, REQS),
        cache_lengths.reshape(1, 1),
        sink_count.reshape(1, 1),
        window_size.reshape(1, 1),
    )


def solution(mesh):
    in_specs = (
        P(None, "req", None, "tp"),
        P(None, "req", None, None, None),
        P(None, "req", None, None, None),
        P(None, "req", None, None),
        P(None, "tp", None),
        P(),
        P(None, "req", "tp"),
        P(None, "tp"),
        P(),
        P("req"),
        P(),
        P(),
        P(),
    )
    out_specs = (P("req", "tp"), P("req", None))
    return jax.shard_map(
        per_device, mesh=mesh, in_specs=in_specs, out_specs=out_specs, check_vma=False
    )
```

```python
import jax
import jax.numpy as jnp
from jax import lax
from jax.experimental import pallas as pl
from jax.experimental.pallas import tpu as pltpu
from jax.sharding import PartitionSpec as P

HEADS = 12
HEAD = 128
KV_HEADS = 2
RESP = 32
CACHE = 384
KEYS = CACHE + RESP
D = 1536

NX, NZ, NC, NT = 4, 16, 2, 4
REQS = NX * NZ * NC
SLOTS = 16
FEAT = D // NT
GROUP = HEADS // NT
VOCAB_BLOCK = 1024
PIECES = 4
PIECE = VOCAB_BLOCK // PIECES
CHUNKS = 4
ROWS = 4 * NX * NC * SLOTS
BLOCK = 512
FEATURE_HALVES = (pl.ds(0, D // 2), pl.ds(D // 2, D // 2))
ALL = pl.ds(0, D)
OWN = 4 * 4 - 1
MESH = pl.DeviceIdType.MESH
EXACT = lax.Precision.HIGHEST


def iota(shape, dim):
    return lax.broadcasted_iota(jnp.int32, shape, dim)


def nt_dot(a, b, precision=None):
    return lax.dot_general(
        a, b, (((1,), (1,)), ((), ())), precision=precision, preferred_element_type=jnp.float32
    )


def fused(
    queries, response_kv, cache_kv, residual, out_proj, gain_in, head, targets_in, lengths_in,
    owner_in, cache_lengths_in, sink_count_in, window_size_in,
    policy_out, scores_out,
    gain, targets, lengths, owner, cache_lengths, sink_count, window_size,
    qbuf, kvbuf, wbuf, resbuf, attbuf, partial,
    hbuf, rows, rs_in, tgt_in, tgt_all, own_all, wanted_buf, select_buf,
    peak_buf, norm_buf, pick_buf, outbuf, in1, ex2, in2, in3,
    load_sem, rs_s, rs_r, tg_s, tg_r, hp_s, hp_r, hq_s, hq_r, hf_s, hf_r,
    z_s, z_r, x_s, x_r, c_s, c_r, e1_s, e1_r, e2_s, e2_r,
):
    req = lax.axis_index("req")
    t = lax.axis_index("tp")
    x = req // (NZ * NC)
    z = (req // NC) % NZ
    c = req % NC
    model = t // 2
    half = t % 2
    pair = t + 1 - 2 * (t % 2)
    across = NT - 1 - t
    group = x * NC + c

    def index_of(px, pz, pc):
        return (px * NZ + pz) * NC + pc

    def send(src, dst, ssem, rsem, preq, pt):
        return pltpu.make_async_remote_copy(
            src_ref=src, dst_ref=dst, send_sem=ssem, recv_sem=rsem,
            device_id={"req": preq, "tp": pt}, device_id_type=MESH,
        )

    barrier = pltpu.get_barrier_semaphore()

    def greet(preq, pt):
        pl.semaphore_signal(
            barrier, inc=1, device_id={"req": preq, "tp": pt}, device_id_type=MESH
        )

    for d in range(1, NX * NC):
        other = (group + d) % (NX * NC)
        greet(index_of(other // NC, z, other % NC), t)
    for d in range(1, NT):
        greet(req, (t + d) % NT)

    def greet_ring(d, carry):
        for e in range(NT):
            greet(index_of(x, (z + d) % NZ, c), (t + e) % NT)
        return carry

    lax.fori_loop(1, NZ, greet_ring, 0)

    kv_lanes = pl.ds(pl.multiple_of((t // 2) * HEAD, HEAD), HEAD)
    slot_start = pl.multiple_of(half * SLOTS, SLOTS)
    loads = [
        pltpu.make_async_copy(queries, qbuf, load_sem.at[0]),
        pltpu.make_async_copy(
            cache_kv.at[:, :, :, kv_lanes], kvbuf.at[:, :, pl.ds(0, CACHE)], load_sem.at[1]
        ),
        pltpu.make_async_copy(
            response_kv.at[:, :, :, kv_lanes], kvbuf.at[:, :, pl.ds(CACHE, RESP)], load_sem.at[2]
        ),
        pltpu.make_async_copy(out_proj, wbuf, load_sem.at[3]),
        pltpu.make_async_copy(residual.at[model, pl.ds(slot_start, SLOTS)], resbuf, load_sem.at[4]),
    ]
    small = [
        (cache_lengths_in, cache_lengths), (sink_count_in, sink_count),
        (window_size_in, window_size), (targets_in, targets), (owner_in, owner),
        (lengths_in, lengths), (gain_in, gain),
    ]
    small = [
        pltpu.make_async_copy(src, dst, load_sem.at[6 + i]) for i, (src, dst) in enumerate(small)
    ]
    own_head = pltpu.make_async_copy(head.at[model], hbuf.at[t], load_sem.at[5])
    for copy in small + loads:
        copy.start()
    own_head.start()

    req_sub = iota((REQS, ROWS), 0)
    row_lane = iota((REQS, ROWS), 1)
    same_xc = ((req_sub >> 5) == (row_lane >> 7)) & ((req_sub & 1) == ((row_lane >> 4) & 1))
    same_z = ((iota((NZ, REQS), 1) >> 1) & (NZ - 1)) == iota((NZ, REQS), 0)
    zmask = jnp.where(same_z, 1.0, 0.0)

    pl.semaphore_wait(barrier, (NX * NC - 1) + (NT * NZ - 1))

    def piece(k):
        return pl.ds(k * PIECE, PIECE)

    def pair_copy(k):
        return send(
            head.at[model, piece(k)], hbuf.at[t, piece(k)], hp_s.at[k], hp_r.at[k], req, pair
        )

    def across_copy(k):
        return send(
            head.at[1 - model, piece(k)], hbuf.at[t, piece(k)], hq_s.at[k], hq_r.at[k],
            req, across,
        )

    def across_recv(k):
        return send(
            head.at[1 - model, piece(k)], hbuf.at[across, piece(k)], hq_s.at[k], hq_r.at[k],
            req, across,
        )

    def forward_copy(k):
        part = hbuf.at[across, piece(k)]
        return send(part, part, hf_s.at[k], hf_r.at[k], req, pair)

    def pair_recv(k):
        part = hbuf.at[pair, piece(k)]
        return send(part, part, hp_s.at[k], hp_r.at[k], req, pair)

    def forward_recv(k):
        part = hbuf.at[NT - 1 - pair, piece(k)]
        return send(part, part, hf_s.at[k], hf_r.at[k], req, pair)

    across_copy(0).start()
    pair_copy(0).start()
    across_copy(1).start()

    for copy in small + loads[:3]:
        copy.wait()
    length = cache_lengths[...]
    stack = (GROUP * RESP, KEYS)
    query_pos = length + (iota(stack, 0) & (RESP - 1))
    key = iota(stack, 1)
    key_pos = jnp.where(key < CACHE, key, length + key - CACHE)
    key_live = (key >= CACHE) | (key < length)
    inside = (key_pos < sink_count[...]) | (query_pos - key_pos < window_size[...])
    allowed = key_live & (key_pos <= query_pos) & inside
    for m in range(2):
        stacked = jnp.concatenate(
            [qbuf[m, 0, :, HEAD * g : HEAD * g + HEAD] for g in range(GROUP)], axis=0
        )
        scores = nt_dot(stacked, kvbuf[m, 0]) * HEAD ** (-0.5)
        masked = jnp.where(allowed, scores, -jnp.inf)
        weights = jnp.exp(masked - jnp.max(masked, axis=-1, keepdims=True))
        weights = (weights / jnp.sum(weights, axis=-1, keepdims=True)).astype(jnp.bfloat16)
        attended = jnp.dot(weights, kvbuf[m, 1], preferred_element_type=jnp.float32)
        attended = attended.astype(jnp.bfloat16)
        for g in range(GROUP):
            attbuf[m, :, HEAD * g : HEAD * g + HEAD] = attended[RESP * g : RESP * g + RESP]
    loads[3].wait()
    for m in range(2):
        partial[m] = jnp.dot(attbuf[m], wbuf[m], preferred_element_type=jnp.float32)

    def rs_copy(d):
        pt = (t + d) % NT
        start = pl.multiple_of((pt % 2) * SLOTS, SLOTS)
        return send(
            partial.at[pt // 2, pl.ds(start, SLOTS)], rs_in.at[d], rs_s.at[d], rs_r.at[d], req, pt
        )

    for d in range(1, NT):
        rs_copy(d).start()

    lane128 = iota((REQS, 128), 1)
    sub128 = iota((REQS, 128), 0)
    same_xc_lane = ((sub128 >> 5) == (lane128 >> 5)) & ((sub128 & 1) == ((lane128 >> 4) & 1))
    wide = jnp.concatenate(
        [zmask * targets[s : s + 1, :].astype(jnp.float32) for s in range(8)], axis=0
    )
    wide = jnp.dot(
        wide, jnp.where(same_xc_lane, 1.0, 0.0), precision=EXACT,
        preferred_element_type=jnp.float32,
    )
    slot_lane = iota((NZ, 128), 1) & (SLOTS - 1)
    placed = jnp.zeros((NZ, 128), jnp.float32)
    for s in range(8):
        placed = jnp.where(slot_lane == s + 8 * half, wide[NZ * s : NZ * s + NZ], placed)
    tgt_in[0] = placed.astype(jnp.int32)

    def tgt_copy(d):
        return send(tgt_in.at[0], tgt_in.at[d], tg_s.at[d], tg_r.at[d], req, (t + d) % NT)

    for d in range(1, NT):
        tgt_copy(d).start()
    own_all[...] = jnp.dot(
        zmask * owner[...].astype(jnp.float32), jnp.where(same_xc, 1.0, 0.0), precision=EXACT,
        preferred_element_type=jnp.float32,
    ).astype(jnp.int32)

    def forward_head(k):
        across_recv(k).wait_recv()
        forward_copy(k).start()
        if k in (1, 2):
            pair_copy(k + 1).start()

    pair_copy(1).start()
    across_copy(2).start()
    forward_head(0)
    across_copy(3).start()

    loads[4].wait()
    hidden = resbuf[...].astype(jnp.float32)
    total = partial[model, pl.ds(slot_start, SLOTS), :]
    for d in range(1, NT):
        rs_copy(d).wait_recv()
        total = total + rs_in[d]
    hidden = hidden + total
    scale_inv = lax.rsqrt(jnp.mean(hidden * hidden, axis=-1, keepdims=True) + 1e-06)
    rows[x, OWN, c] = (hidden * scale_inv * gain[pl.ds(model, 1), :]).astype(jnp.bfloat16)

    steps = range(1, 5)
    streams = [(side, j) for side in range(2) for j in range(2)]

    def slot_of(k, side, j):
        return 4 * (k - 1) + 2 * side + j

    def exists(k, side, j):
        return slot_of(k, side, j) != OWN

    def away(side, hops):
        return index_of(x, (z + hops) % NZ if side == 0 else (z + NZ - hops) % NZ, c)

    targets_of = [[away(side, 1), away(side, 2)] for side in range(2)]

    def z_copy(k, side, j):
        src = OWN if k == 1 else slot_of(k - 1, side, j)
        dst = slot_of(k, side, j)
        to = targets_of[side][j if k == 1 else 1]
        return send(rows.at[x, src, c], rows.at[x, dst, c], z_s.at[dst], z_r.at[dst], to, t)

    beside = [index_of((x + d) % NX, z, c) for d in range(NX)]
    twin = index_of(x, z, 1 - c)

    groups = [(OWN, 1)] + [(4 * (k - 1) + 2 * side, 2) for k in steps for side in range(2)]
    groups[8] = (OWN - 1, 1)

    def x_part(g, block, part_lanes):
        start, size = groups[g]
        return rows.at[(x + block) % NX, pl.ds(start, size), c, :, part_lanes]

    def x_copy(g, way, second, receiving=False):
        back = NX - 1 if way == 0 else 1
        block = (back if second else 0) + (back if receiving else 0)
        part = x_part(g, block, FEATURE_HALVES[way] if second else ALL)
        n = 4 * g + 2 * second + way
        return send(part, part, x_s.at[n], x_r.at[n], beside[1 if way == 0 else NX - 1], t)

    def twin_copy(g, core):
        start, size = groups[g]
        part = rows.at[:, pl.ds(start, size), core]
        return send(part, part, c_s.at[g], c_r.at[g], twin, t)

    def x_send(g):
        for way in range(2):
            x_copy(g, way, 0).start()

    def x_pass(g):
        for way in range(2):
            x_copy(g, way, 0, True).wait_recv()
            x_copy(g, way, 1).start()

    def x_done(g):
        for way in range(2):
            x_copy(g, way, 1, True).wait_recv()
        twin_copy(g, c).start()

    def other_core(*gs):
        for g in gs:
            twin_copy(g, 1 - c).wait_recv()

    def arrive(k):
        for side in range(2):
            for j in range(2):
                if not exists(k, side, j):
                    continue
                z_copy(k, side, j).wait_recv()
                if k < 4 and exists(k + 1, side, j):
                    z_copy(k + 1, side, j).start()
            x_send(2 * k - 1 + side)

    for j in range(2):
        for side in range(2):
            z_copy(1, side, j).start()
    x_send(0)
    forward_head(1)

    tgt_own = jnp.zeros((NZ, 128), jnp.int32)
    for d in range(NT):
        if d:
            tgt_copy(d).wait_recv()
        wanted_half = ((t + NT - d) % NT) // 2 == half
        tgt_own = tgt_own + jnp.where(wanted_half, tgt_in[d], 0)
    small_lane = ((iota((128, ROWS), 1) >> 7) << 5) + (iota((128, ROWS), 1) & 31)
    repeat = jnp.where(small_lane == iota((128, ROWS), 0), 1.0, 0.0)
    tgt_wide = jnp.dot(
        tgt_own.astype(jnp.float32), repeat, precision=EXACT, preferred_element_type=jnp.float32
    )
    tgt_all[...] = tgt_wide.astype(jnp.int32) - req * VOCAB_BLOCK
    outbuf[...] = jnp.zeros_like(outbuf)
    peak_buf[...] = jnp.full_like(peak_buf, -jnp.inf)
    norm_buf[...] = jnp.zeros_like(norm_buf)
    pick_buf[...] = jnp.zeros_like(pick_buf)

    def prepare(k):
        near, far = 2 * k + 1, 2 * k + 2
        places = [(z + NZ - near) % NZ, (z + NZ - far) % NZ, (z + near) % NZ, (z + far % 8) % NZ]
        place = (iota((1, ROWS), 1) >> 5) & 3

        def pick(table):
            found = table[pl.ds(places[3], 1), :]
            for i in range(3):
                found = jnp.where(place == i, table[pl.ds(places[i], 1), :], found)
            return found

        wanted_buf[k] = pick(tgt_all)
        sub = iota((REQS, ROWS), 0)
        dest = ((sub >> 5) * NZ + (sub & (NZ - 1))) * NC + ((sub >> 4) & 1)
        select_buf[k] = jnp.where(dest == pick(own_all), 1.0, 0.0).astype(jnp.bfloat16)

    def head_ready(k):
        pair_recv(k).wait_recv()
        forward_recv(k).wait_recv()

    def units(k0, k1, p0, p1):
        def unit(i, carry):
            k = k0 + i // (p1 - p0)
            p = p0 + i % (p1 - p0)
            base = pl.multiple_of(p * BLOCK, BLOCK)
            chunk = rows[:, pl.ds(4 * k, 4)].reshape(ROWS, D)
            block = [hbuf[q, pl.ds(base, BLOCK), :] for q in range(NT)]
            logits = nt_dot(jnp.concatenate(block, axis=1), chunk)
            peak = jnp.max(logits, axis=0, keepdims=True)
            hit = iota((BLOCK, ROWS), 0) == wanted_buf[k] - base
            pick_buf[k] += jnp.sum(jnp.where(hit, logits, 0.0), axis=0, keepdims=True)
            old = peak_buf[k]
            new = jnp.maximum(old, peak)
            norm = jnp.sum(jnp.exp(logits - new), axis=0, keepdims=True)
            norm_buf[k] = norm_buf[k] * jnp.exp(old - new) + norm
            peak_buf[k] = new
            return carry

        lax.fori_loop(0, (k1 - k0) * (p1 - p0), unit, 0)

    arrive(1)
    x_pass(0)
    forward_head(2)
    prepare(0)
    prepare(1)

    arrive(2)
    x_pass(1)
    x_pass(2)
    x_done(0)
    forward_head(3)
    prepare(2)
    prepare(3)

    arrive(3)
    x_pass(3)
    x_pass(4)
    x_done(1)
    x_done(2)
    own_head.wait()
    head_ready(0)
    head_ready(1)

    arrive(4)
    x_pass(5)
    x_pass(6)
    x_done(3)
    x_done(4)
    other_core(1, 2)
    units(0, 1, 0, 1)
    x_pass(7)
    x_pass(8)
    x_done(5)
    x_done(6)
    other_core(3, 4)
    units(1, 2, 0, 1)
    x_done(7)
    x_done(8)
    other_core(5, 6)
    units(2, 3, 0, 1)
    head_ready(2)
    head_ready(3)
    units(0, 3, 1, 2)
    def finish(k, carry):
        sub = iota((2 * SLOTS, ROWS), 0)
        slot = iota((2 * SLOTS, ROWS), 1) & (SLOTS - 1)
        lse = peak_buf[k] + jnp.log(norm_buf[k])
        values = jnp.where(sub == slot, lse, jnp.where(sub == slot + SLOTS, pick_buf[k], 0.0))
        terms = []
        for _ in range(3):
            terms.append(values.astype(jnp.bfloat16))
            values = values - terms[-1].astype(jnp.float32)
        terms.append(jnp.zeros_like(terms[0]))
        outbuf[...] += nt_dot(select_buf[k], jnp.concatenate(terms, axis=0))
        return carry

    lax.fori_loop(0, 3, finish, 0)
    other_core(7, 8, 0)
    units(3, 4, 0, 2)
    finish(3, 0)
    found = outbuf[...]
    outbuf[...] = (found + pltpu.roll(found, 96, 1)) + pltpu.roll(found, 64, 1)

    def e1_copy(d):
        other = (group + d) % (NX * NC)
        return send(
            outbuf.at[pl.ds(pl.multiple_of(other * NZ, NZ), NZ)], in1.at[d], e1_s.at[d], e1_r.at[d],
            index_of(other // NC, z, other % NC), t,
        )

    for d in range(1, NX * NC):
        e1_copy(d).start()
    in1[0] = outbuf[pl.ds(pl.multiple_of(group * NZ, NZ), NZ), :]
    for d in range(1, NX * NC):
        e1_copy(d).wait_recv()

    def combine(values):
        peak = jnp.max(values, axis=0, keepdims=True)
        lse = peak + jnp.log(jnp.sum(jnp.exp(values - peak), axis=0, keepdims=True))
        pick = jnp.sum(values, axis=0, keepdims=True)
        return jnp.where(iota(lse.shape, 2) < SLOTS, lse, pick)[0]

    merged = combine(in1[...])
    for k in range(NZ):
        ex2[k] = merged[k : k + 1]

    def e2_copy(d, e):
        pz = (z + d) % NZ
        n = NT * d + e
        return send(
            ex2.at[pz], in2.at[t, d], e2_s.at[n], e2_r.at[n], index_of(x, pz, c), (t + e) % NT
        )

    def e2_recv(d, e):
        n = NT * d + e
        dst = in2.at[(t + NT - e) % NT, d]
        return send(ex2.at[0], dst, e2_s.at[n], e2_r.at[n], index_of(x, (z + d) % NZ, c), (t + e) % NT)

    def ring_loop(body):
        def step(d, carry):
            for e in range(NT):
                body(d, e)
            return carry

        for e in range(1, NT):
            body(0, e)
        lax.fori_loop(1, NZ, step, 0)

    ring_loop(lambda d, e: e2_copy(d, e).start())
    in2[t, 0] = ex2[z]
    count = jnp.sum(jnp.where(owner[...] == req, lengths[...], 0), axis=1, keepdims=True)
    ring_loop(lambda d, e: e2_recv(d, e).wait_recv())
    for column in range(NT):
        final = combine(in2[column])
        in3[column] = pltpu.roll(final, 128 - SLOTS, 1) - final
    lane = iota((1, 128), 1)
    live0 = (lane < SLOTS) & (lane < count)
    live1 = (lane < SLOTS) & (lane + SLOTS < count)
    low, high = in3[0], in3[1]
    policy_total = jnp.sum(
        jnp.where(live0, low, 0.0) + jnp.where(live1, high, 0.0), axis=1, keepdims=True
    )
    ratio_total = jnp.sum(
        jnp.where(live0, low - in3[2], 0.0) + jnp.where(live1, high - in3[3], 0.0),
        axis=1, keepdims=True,
    )
    counts = count.astype(jnp.float32)
    scores = jnp.where(lane == 0, policy_total / counts, ratio_total / counts)
    scores_out[...] = scores[:, 0:2]
    mine = in3[t // 2]
    mine = jnp.where(half == 1, pltpu.roll(mine, 120, 1), mine)
    mine = jnp.where(lane + 8 * t < count, mine, 0.0)
    policy_out[...] = mine[:, 0:8]

    for d in range(1, NT):
        rs_copy(d).wait_send()
        tgt_copy(d).wait_send()
    for k in steps:
        for side, j in streams:
            if exists(k, side, j):
                z_copy(k, side, j).wait_send()
    for g in range(9):
        for way in range(2):
            x_copy(g, way, 0).wait_send()
            x_copy(g, way, 1).wait_send()
        twin_copy(g, c).wait_send()

    def head_sent(k, carry):
        pair_copy(k).wait_send()
        across_copy(k).wait_send()
        forward_copy(k).wait_send()
        return carry

    lax.fori_loop(0, PIECES, head_sent, 0)

    for d in range(1, NX * NC):
        e1_copy(d).wait_send()
    ring_loop(lambda d, e: e2_copy(d, e).wait_send())


def per_device(
    queries,
    response_kv,
    cache_kv,
    residual,
    out_proj,
    norm_gain,
    lm_head,
    targets,
    resp_lengths,
    cache_lengths,
    owner_slot,
    sink_count,
    window_size,
):
    dma = pltpu.SemaphoreType.DMA
    vmem = pl.BlockSpec(memory_space=pltpu.VMEM)
    hbm = pl.BlockSpec(memory_space=pltpu.HBM)
    semaphores = [13] + [NT] * 4 + [PIECES] * 6 + [16] * 2 + [36] * 2
    semaphores += [9] * 2 + [8] * 2 + [NZ * NT] * 2
    bf16, f32, i32 = jnp.bfloat16, jnp.float32, jnp.int32
    return pl.pallas_call(
        fused,
        out_shape=(jax.ShapeDtypeStruct((1, 8), f32), jax.ShapeDtypeStruct((1, 2), f32)),
        in_specs=[hbm] * 13,
        out_specs=(vmem, vmem),
        scratch_shapes=[
            pltpu.VMEM((2, D), f32),
            pltpu.VMEM((RESP // NT, REQS), i32),
            pltpu.VMEM((1, REQS), i32),
            pltpu.VMEM((1, REQS), i32),
            pltpu.VMEM((1, 1), i32),
            pltpu.VMEM((1, 1), i32),
            pltpu.VMEM((1, 1), i32),
            pltpu.VMEM((2, 1, RESP, FEAT), bf16),
            pltpu.VMEM((2, 2, KEYS, HEAD), bf16),
            pltpu.VMEM((2, FEAT, D), bf16),
            pltpu.VMEM((SLOTS, D), bf16),
            pltpu.VMEM((2, RESP, FEAT), bf16),
            pltpu.VMEM((2, RESP, D), f32),
            pltpu.VMEM((NT, VOCAB_BLOCK, FEAT), bf16),
            pltpu.VMEM((NX, NZ, NC, SLOTS, D), bf16),
            pltpu.VMEM((NT, SLOTS, D), f32),
            pltpu.VMEM((NT, NZ, 128), i32),
            pltpu.VMEM((NZ, ROWS), i32),
            pltpu.VMEM((NZ, ROWS), i32),
            pltpu.VMEM((CHUNKS, 1, ROWS), i32),
            pltpu.VMEM((CHUNKS, REQS, ROWS), bf16),
            pltpu.VMEM((CHUNKS, 1, ROWS), f32),
            pltpu.VMEM((CHUNKS, 1, ROWS), f32),
            pltpu.VMEM((CHUNKS, 1, ROWS), f32),
            pltpu.VMEM((REQS, 128), f32),
            pltpu.VMEM((NX * NC, NZ, 128), f32),
            pltpu.VMEM((NZ, 1, 128), f32),
            pltpu.VMEM((NT, NZ, 1, 128), f32),
            pltpu.VMEM((NT, 1, 128), f32),
        ]
        + [dma((n,)) for n in semaphores],
        compiler_params=pltpu.CompilerParams(
            collective_id=0, has_side_effects=True, vmem_limit_bytes=63 << 20
        ),
    )(
        queries,
        response_kv.reshape(2, 2, RESP, KV_HEADS * HEAD),
        cache_kv.reshape(2, 2, CACHE, KV_HEADS * HEAD),
        residual.reshape(2, RESP, D),
        out_proj,
        norm_gain,
        lm_head,
        targets.T,
        resp_lengths.reshape(1, REQS),
        owner_slot.reshape(1, REQS),
        cache_lengths.reshape(1, 1),
        sink_count.reshape(1, 1),
        window_size.reshape(1, 1),
    )


def solution(mesh):
    in_specs = (
        P(None, "req", None, "tp"),
        P(None, "req", None, None, None),
        P(None, "req", None, None, None),
        P(None, "req", None, None),
        P(None, "tp", None),
        P(),
        P(None, "req", "tp"),
        P(None, "tp"),
        P(),
        P("req"),
        P(),
        P(),
        P(),
    )
    out_specs = (P("req", "tp"), P("req", None))
    return jax.shard_map(
        per_device, mesh=mesh, in_specs=in_specs, out_specs=out_specs, check_vma=False
    )
```
